256 devices in a mesh: sub: 64 (over x, z, core), col: 4 (over y).
Axes of the slice: x: 4, y: 4, z: 8, core: 2. Of those that a mesh axis runs over, the one named last changes fastest.
Arguments:
- flexibility: bfloat16 [64, 768, 768], P('sub')
- omega: bfloat16 [256, 24576], P('col', 'sub'), may hold values from -6 to 6
- block_row: int32 [64, 6], replicated, may hold values from 0 to 191, as said below
- block_sign: int32 [64, 6], replicated, may hold values from -1 to 1, as said below
Outputs:
- sketch: float32 [256, 24576], P('col', 'sub')
- basis: float32 [256, 24576], P('col', 'sub')
- factor: float32 [256, 256], replicated
The draws below stay inside these ranges and needn't reach their ends.
Inputs may be any that keep to these rules, and one draw needn't show every extreme that they name: `block_row`: each row block is named by exactly two entries, one whose block_sign is 1 and one whose block_sign is -1. Row block b lies in the sketch columns of sub index b // 3. For any two sub indices p and q, the blocks of p's one substructure name row blocks of q either exactly 2 times or never. `block_sign`: every entry is -1 or 1.
All inputs are finite; a program needn't handle non-finite values.
Results may differ from the reference program's by a relative error of at most 0.0003.
Values may be sent and summed in bfloat16 or wider, within the bound.
A program may use at most 64 MiB of HBM per device.

```python
import math
import jax
import jax.numpy as jnp
from jax import lax

S_DEV = 1
LB = 6
BLK = 128
K = 256
LDOF = 768
S_TOTAL = 64
RB_DEV = 3
RB_TOTAL = 192
ROWS = 24576
CAP = 2
N_SUB = 64


def build_map(key):
    base = jax.random.fold_in(key, 11)
    key_offsets = jax.random.fold_in(base, 1)
    key_first = jax.random.fold_in(base, 2)
    key_second = jax.random.fold_in(base, 3)
    key_pairing = jax.random.fold_in(base, 4)
    key_order = jax.random.fold_in(base, 5)
    ref_count = S_DEV * LB
    groups = ref_count // CAP
    offsets = jax.random.permutation(key_offsets, N_SUB)[:groups]
    first_perm = jax.random.permutation(key_first, N_SUB)
    second_perm = jax.random.permutation(key_second, N_SUB)
    slots = jnp.arange(ref_count, dtype=jnp.int32)
    senders = jnp.arange(N_SUB, dtype=jnp.int32)[:, None]
    owners = second_perm[(first_perm[senders] + offsets[slots // CAP][None, :]) % N_SUB]
    table = jnp.tile(slots[None, :], (N_SUB, 1))
    pairing = jax.random.permutation(key_pairing, table, axis=1, independent=True)
    placed = pairing[owners, jnp.broadcast_to(slots[None, :], owners.shape)]
    rows = owners * RB_DEV + placed // 2
    signs = 1 - 2 * (placed % 2)
    order = jax.random.permutation(key_order, table, axis=1, independent=True)
    rows = jnp.take_along_axis(rows, order, axis=1).reshape(N_SUB * S_DEV, LB)
    signs = jnp.take_along_axis(signs, order, axis=1).reshape(N_SUB * S_DEV, LB)
    return (rows.astype(jnp.int32), signs.astype(jnp.int32))


def draw_block_row(key, part):
    return build_map(key)[0]


def draw_block_sign(key, part):
    return build_map(key)[1]


def draw_flexibility(key, part):
    key_off = jax.random.fold_in(key, 21)
    key_diag = jax.random.fold_in(key, 22)
    shape = (S_TOTAL, LDOF, LDOF)
    raw = jax.random.normal(key_off, shape, jnp.float32)
    diagonal = jax.random.uniform(key_diag, (S_TOTAL, LDOF), jnp.float32, 0.75, 1.5)
    off_part = (raw + jnp.swapaxes(raw, 1, 2)) * (0.3 / math.sqrt(2.0 * LDOF))
    index = jnp.arange(LDOF)
    on_diagonal = (index[:, None] == index[None, :])[None, :, :]
    whole = jnp.where(on_diagonal, diagonal[:, :, None], off_part)
    return whole.astype(jnp.bfloat16)


def steps_of(key, extent, pieces, least, top_value):
    gain, own = 1.0, jax.random.fold_in(key, 6)
    for dim, shards_of in pieces:
        heights = jnp.exp(jax.random.uniform(jax.random.fold_in(own, dim), (shards_of,), jnp.float32, least / len(pieces), top_value / len(pieces)))
        gain = gain * jnp.repeat(heights, extent[dim] // shards_of).reshape([-1 if axis == dim else 1 for axis in range(len(extent))])
    return gain


def normal_values(stream_key, dims, width, bound, pieces=(), held_as=jnp.bfloat16):
    gain = steps_of(stream_key, dims, pieces, -0.22, 0.18) if pieces else 1.0
    values = jax.random.normal(stream_key, dims, jnp.float32) * width * gain
    return jnp.minimum(jnp.maximum(values, -bound), bound).astype(held_as)


def setup_inputs(seed: int = 0) -> dict:
    seeds = jax.random.split(jax.random.key(seed), 5)
    return {
        "flexibility": draw_flexibility(jax.random.fold_in(seeds[4], 71), 0),
        "omega": normal_values(seeds[1], (K, ROWS), 1.0, 6.0, ((0, 4), (1, 64))),
        "block_row": draw_block_row(jax.random.fold_in(seeds[4], 71), 0),
        "block_sign": draw_block_sign(jax.random.fold_in(seeds[4], 71), 0),
    }


def reference(flexibility, omega, block_row, block_sign):
    blocks = omega.reshape(K, RB_TOTAL, BLK)

    def accumulate(total, inputs):
        matrix, rows, signs = inputs
        signed = jnp.take(blocks, rows, axis=1) * signs.astype(omega.dtype)[None, :, None]
        response = jnp.dot(signed.reshape(K, LB * BLK).astype(jnp.float32), matrix.T.astype(jnp.float32), preferred_element_type=jnp.float32)
        shaped = response.reshape(K, LB, BLK) * signs.astype(jnp.float32)[None, :, None]
        return (total.at[:, rows].add(shaped), None)
    zeros = jnp.zeros((K, RB_TOTAL, BLK), jnp.float32)
    total, ignored = lax.scan(accumulate, zeros, (flexibility, block_row, block_sign))
    sketch = total.reshape(K, ROWS)
    gram = jnp.dot(sketch, sketch.T, precision=lax.Precision.HIGHEST) / ROWS
    upper = jnp.linalg.cholesky(gram).T
    inverse = lax.linalg.triangular_solve(upper, jnp.eye(K, dtype=gram.dtype), left_side=True, lower=False)
    basis = jnp.dot(inverse.T, sketch, precision=lax.Precision.HIGHEST)
    return (sketch, basis, upper)
```

```python
import functools

import jax
import jax.numpy as jnp
from jax import lax
from jax.experimental import pallas as pl
from jax.experimental.pallas import tpu as pltpu
from jax.sharding import PartitionSpec as P

F32 = jnp.float32
BF16 = jnp.bfloat16
NN = (((1,), (0,)), ((), ()))
NT = (((1,), (1,)), ((), ()))


def mm1(a, b, dims=NN):
    return lax.dot_general(a.astype(BF16), b.astype(BF16), dims, preferred_element_type=F32)


def halves(a):
    high = a.astype(BF16)
    return high, (a - high.astype(F32)).astype(BF16)


def mm3(a, b, dims=NN):
    ah, al = halves(a)
    bh, bl = halves(b)
    dot = functools.partial(lax.dot_general, dimension_numbers=dims, preferred_element_type=F32)
    return dot(ah, bh) + (dot(ah, bl) + dot(al, bh))


def finish_kernel(full_ref, gram_ref, basis_ref, upper_ref, work, lower):
    order = gram_ref.shape[0]
    rows = basis_ref.shape[0]
    i_row = lax.broadcasted_iota(jnp.int32, (order, order), 0)
    i_col = lax.broadcasted_iota(jnp.int32, (order, order), 1)
    eye = jnp.where(i_row == i_col, 1.0, 0.0).astype(F32)
    phi_mask = jnp.where(i_row > i_col, 1.0, 0.5 * eye).astype(F32)
    gram = gram_ref[...]
    on_diag = gram * eye
    d_row = jnp.sum(on_diag, axis=0, keepdims=True)
    d_col = jnp.sum(on_diag, axis=1, keepdims=True)
    s_row = lax.rsqrt(d_row)
    s_col = lax.rsqrt(d_col)
    err = jnp.where(i_row == i_col, 0.0, gram * s_row * s_col)
    p = err * phi_mask
    n = mm1(p, p, NT) * phi_mask + mm1(p, p) - p
    z = err + n + mm1(n, err)
    resid = z + n.T + mm1(z, n, NT)
    p = resid * phi_mask
    n = n - p - mm1(p, n)
    z = err + n + mm3(n, err)
    resid = z + n.T + mm3(z, n, NT)
    p = resid * phi_mask
    n = n - p - mm1(p, n)
    miss = jnp.sum(resid * resid)
    z = err + n + mm3(n, err)
    upper_ref[...] = jnp.where(i_row <= i_col, (eye + z) * (d_row * s_row), 0.0)
    lower[...] = jnp.where(i_row >= i_col, (eye + n) * s_row, 0.0)

    @pl.when(jnp.logical_not(miss < 4e-6))
    def eliminate():
        work[...] = gram
        lower[...] = eye
        lane = lax.broadcasted_iota(jnp.int32, (1, order), 1)
        sub = lax.broadcasted_iota(jnp.int32, (order, 1), 0)

        @pl.loop(0, order)
        def step(j):
            remain = work[...]
            row = work[pl.ds(j, 1), :]
            pivot = jnp.sum(jnp.where(lane == j, row, 0.0), axis=1, keepdims=True)
            scale = 1.0 / jnp.sqrt(pivot)
            u_row = jnp.where(lane >= j, row * scale, 0.0)
            column = jnp.sum(jnp.where(i_col == j, remain, 0.0), axis=1, keepdims=True)
            column = jnp.where(sub > j, column * scale, 0.0)
            l_row = lower[pl.ds(j, 1), :] * scale
            upper_ref[pl.ds(j, 1), :] = u_row
            work[...] = remain - column * u_row
            below = lower[...] - column * l_row
            lower[...] = jnp.where(sub == j, l_row, below)

    mine = pl.ds(pl.multiple_of(lax.axis_index("col") * rows, rows), rows)
    basis_ref[...] = mm3(lower[mine, :], full_ref[...])


def finish(full, gram, rows):
    order, width = full.shape
    return pl.pallas_call(
        finish_kernel,
        out_shape=(
            jax.ShapeDtypeStruct((rows, width), F32),
            jax.ShapeDtypeStruct((order, order), F32),
        ),
        in_specs=[pl.BlockSpec(memory_space=pltpu.VMEM)] * 2,
        out_specs=(pl.BlockSpec(memory_space=pltpu.VMEM),) * 2,
        scratch_shapes=[pltpu.VMEM((order, order), F32)] * 2,
        name="factor_and_basis",
    )(full, gram)


def exchange(x):
    return lax.all_to_all(x, "sub", split_axis=0, concat_axis=0, tiled=True)


def shards(flexibility, omega, block_row, block_sign):
    sub_count = lax.axis_size("sub")
    position = lax.axis_index("sub")
    local_dofs = flexibility.shape[1]
    local_blocks = block_row.shape[1]
    block_len = local_dofs // local_blocks
    col_width, row_count = omega.shape
    owned = row_count // block_len
    blocks = sub_count * owned
    refs = sub_count * local_blocks
    pick = block_row.reshape(refs, 1) == jnp.arange(blocks)[None, :]
    pick = pick.astype(F32) * block_sign.reshape(refs, 1).astype(F32)
    row_omega = exchange(omega).reshape(blocks, block_len)
    wanted = jnp.dot(pick.astype(BF16), row_omega, preferred_element_type=F32).astype(BF16)
    signed = exchange(wanted.reshape(sub_count, local_dofs))
    response = lax.dot_general(signed, flexibility[0], NT, preferred_element_type=F32)
    contrib = exchange(response).reshape(refs, block_len)
    total = lax.dot_general(pick, contrib, (((0,), (0,)), ((), ())), precision=lax.Precision.HIGHEST)
    sketch = exchange(total.reshape(sub_count, row_count))
    full = lax.all_gather(sketch, "col", axis=0, tiled=True)
    part = lax.dot_general(sketch, full, NT, precision=lax.Precision.HIGHEST) / (row_count * sub_count)
    mine = jnp.sum(exchange(part), axis=0, keepdims=True)
    gram = lax.all_gather(lax.all_gather(mine, "sub", axis=0, tiled=True), "col", axis=0, tiled=True)
    basis, upper = finish(full, gram, col_width)
    return (sketch, basis, upper)


def solution(mesh):
    placed = (P("sub", None, None), P("col", "sub"), P(), P())
    return jax.shard_map(
        shards,
        mesh=mesh,
        in_specs=placed,
        out_specs=(P("col", "sub"), P("col", "sub"), P()),
        check_vma=False,
    )
```

```python
import functools

import jax
import jax.numpy as jnp
from jax import lax
from jax.experimental import pallas as pl
from jax.experimental.pallas import tpu as pltpu
from jax.sharding import PartitionSpec as P

F32 = jnp.float32
BF16 = jnp.bfloat16
NN = (((1,), (0,)), ((), ()))
NT = (((1,), (1,)), ((), ()))


def mm1(a, b, dims=NN):
    return lax.dot_general(a.astype(BF16), b.astype(BF16), dims, preferred_element_type=F32)


def halves(a):
    high = a.astype(BF16)
    return high, (a - high.astype(F32)).astype(BF16)


def mm3(a, b, dims=NN):
    ah, al = halves(a)
    bh, bl = halves(b)
    dot = functools.partial(lax.dot_general, dimension_numbers=dims, preferred_element_type=F32)
    return dot(ah, bh) + (dot(ah, bl) + dot(al, bh))


def finish_kernel(full_ref, gram_ref, sketch_ref, basis_ref, upper_ref, work, lower):
    order = gram_ref.shape[0]
    rows = basis_ref.shape[0]
    i_row = lax.broadcasted_iota(jnp.int32, (order, order), 0)
    i_col = lax.broadcasted_iota(jnp.int32, (order, order), 1)
    eye = jnp.where(i_row == i_col, 1.0, 0.0).astype(F32)
    phi_mask = jnp.where(i_row > i_col, 1.0, 0.5 * eye).astype(F32)
    gram = gram_ref[...]
    on_diag = gram * eye
    d_row = jnp.sum(on_diag, axis=0, keepdims=True)
    d_col = jnp.sum(on_diag, axis=1, keepdims=True)
    s_row = lax.rsqrt(d_row)
    s_col = lax.rsqrt(d_col)
    err = jnp.where(i_row == i_col, 0.0, gram * s_row * s_col)
    p = err * phi_mask
    n = mm1(p, p, NT) * phi_mask + mm1(p, p) - p
    z = err + n + mm1(n, err)
    resid = z + n.T + mm1(z, n, NT)
    p = resid * phi_mask
    n = n - p - mm1(p, n)
    z = err + n + mm3(n, err)
    resid = z + n.T + mm3(z, n, NT)
    p = resid * phi_mask
    n = n - p - mm1(p, n)
    miss = jnp.sum(resid * resid)
    z = err + n + mm3(n, err)
    upper_ref[...] = jnp.where(i_row <= i_col, (eye + z) * (d_row * s_row), 0.0)
    lower[...] = jnp.where(i_row >= i_col, (eye + n) * s_row, 0.0)

    @pl.when(jnp.logical_not(miss < 4e-6))
    def eliminate():
        work[...] = gram
        lower[...] = eye
        lane = lax.broadcasted_iota(jnp.int32, (1, order), 1)
        sub = lax.broadcasted_iota(jnp.int32, (order, 1), 0)

        @pl.loop(0, order)
        def step(j):
            remain = work[...]
            row = work[pl.ds(j, 1), :]
            pivot = jnp.sum(jnp.where(lane == j, row, 0.0), axis=1, keepdims=True)
            scale = 1.0 / jnp.sqrt(pivot)
            u_row = jnp.where(lane >= j, row * scale, 0.0)
            column = jnp.sum(jnp.where(i_col == j, remain, 0.0), axis=1, keepdims=True)
            column = jnp.where(sub > j, column * scale, 0.0)
            l_row = lower[pl.ds(j, 1), :] * scale
            upper_ref[pl.ds(j, 1), :] = u_row
            work[...] = remain - column * u_row
            below = lower[...] - column * l_row
            lower[...] = jnp.where(sub == j, l_row, below)

    mine = pl.ds(pl.multiple_of(lax.axis_index("col") * rows, rows), rows)
    basis_ref[...] = mm3(lower[mine, :], full_ref[...])
    sketch_ref[...] = full_ref[mine, :]


def finish(full, gram, rows):
    order, width = full.shape
    return pl.pallas_call(
        finish_kernel,
        out_shape=(
            jax.ShapeDtypeStruct((rows, width), F32),
            jax.ShapeDtypeStruct((rows, width), F32),
            jax.ShapeDtypeStruct((order, order), F32),
        ),
        in_specs=[pl.BlockSpec(memory_space=pltpu.VMEM)] * 2,
        out_specs=(pl.BlockSpec(memory_space=pltpu.VMEM),) * 3,
        scratch_shapes=[pltpu.VMEM((order, order), F32)] * 2,
        name="factor_and_basis",
    )(full, gram)


MESH = pl.DeviceIdType.MESH
TN = (((0,), (0,)), ((), ()))


def stack_lanes(x, length):
    return jnp.concatenate([x[:, k : k + length] for k in range(0, x.shape[1], length)], axis=0)


def spread_rows(x, parts):
    length = x.shape[0] // parts
    return jnp.concatenate([x[k * length : (k + 1) * length] for k in range(parts)], axis=1)


def sketch_kernel(
    n, m, omega_ref, flex_ref, row_ref, sign_ref, full_ref, gram_ref,
    spare, flex, a_src, a_dst, b_src, b_dst, c_src, c_dst, d_src, full, g_src, g_dst, h_src, gram,
    flex_sem, send, recv,
):
    me = lax.axis_index("sub")
    col = lax.axis_index("col")
    rows, width = a_src.shape
    refs = row_ref.shape[0]
    length = b_src.shape[1] // refs
    owned = width // length

    load = pltpu.make_async_copy(flex_ref, flex, flex_sem)
    load.start()

    barrier = pltpu.get_barrier_semaphore()

    def greet(k, carry):
        pl.semaphore_signal(
            barrier, inc=1, device_id={"sub": lax.rem(me + k, n)}, device_id_type=MESH
        )
        return carry

    lax.fori_loop(1, n, greet, 0)
    for k in range(1, m):
        pl.semaphore_signal(
            barrier, inc=1, device_id={"col": lax.rem(col + k, m)}, device_id_type=MESH
        )
    a_src[...] = omega_ref[...].astype(F32)
    pl.semaphore_wait(barrier, n - 1 + m - 1)

    def start(phase, source, target):
        own = pltpu.make_async_copy(source(me), target, recv.at[phase])
        own.start()
        pltpu.make_async_copy(
            source(me), spare.at[phase, :, pl.ds(0, target.shape[1])], send.at[phase]
        ).start()

        def put(k, carry):
            peer = lax.rem(me + k, n)
            pltpu.make_async_remote_copy(
                src_ref=source(peer), dst_ref=target, send_sem=send.at[phase],
                recv_sem=recv.at[phase], device_id={"sub": peer}, device_id_type=MESH,
            ).start()
            return carry

        lax.fori_loop(1, n, put, 0)

    def arrive(phase, whole):
        pltpu.make_async_copy(whole, whole, recv.at[phase]).wait()

    def start_col(phase, ref):
        for k in range(1, m):
            pltpu.make_async_remote_copy(
                src_ref=ref.at[col], dst_ref=ref.at[col], send_sem=send.at[phase],
                recv_sem=recv.at[phase], device_id={"col": lax.rem(col + k, m)},
                device_id_type=MESH,
            ).start()

    def row_of(ref):
        return lambda r: ref.at[pl.ds(r, 1), :]

    start(0, row_of(a_src), a_dst.at[pl.ds(me, 1), :])
    spot = lax.broadcasted_iota(jnp.int32, (owned * n, n), 0)
    piece = sum([jnp.where(spot >= n * j, 1, 0) for j in range(1, owned)])
    named = owned * (spot - n * piece) + piece
    pick = jnp.concatenate(
        [
            jnp.where(row_ref[l : l + 1, :] == named, sign_ref[l : l + 1, :], 0).astype(F32)
            for l in range(refs)
        ],
        axis=1,
    ).astype(BF16)
    arrive(0, a_dst)
    wanted = lax.dot_general(
        pick, stack_lanes(a_dst[...], length).astype(BF16), TN, preferred_element_type=F32
    )
    b_src[...] = spread_rows(wanted, refs)

    start(1, row_of(b_src), b_dst.at[pl.ds(me, 1), :])
    load.wait()
    arrive(1, b_dst)
    c_src[...] = lax.dot_general(
        b_dst[...].astype(BF16), flex[...], NT, preferred_element_type=F32
    )

    start(2, row_of(c_src), c_dst.at[pl.ds(me, 1), :])
    arrive(2, c_dst)
    terms = stack_lanes(c_dst[...], length)
    high, rest = halves(terms)
    middle, low = halves(terms - high.astype(F32))
    total = sum(
        [lax.dot_general(pick, t, NN, preferred_element_type=F32) for t in (low, middle, high)]
    )
    d_src[...] = spread_rows(total, owned)

    start(3, row_of(d_src), full.at[col, pl.ds(me, 1), :])
    arrive(3, full.at[col])
    start_col(4, full)
    arrive(4, full.at[pl.ds(0, m - 1)])
    whole = full[...].reshape(m * rows, width)
    full_ref[...] = whole
    g_src[...] = mm3(full[col], whole, NT)

    start(5, row_of(g_src), g_dst.at[pl.ds(me, 1), :])
    arrive(5, g_dst)
    h_src[...] = jnp.sum(g_dst[...], axis=0, keepdims=True) / (width * n)

    start(6, lambda r: h_src, gram.at[col, pl.ds(me, 1), :])
    arrive(6, gram.at[col])
    start_col(7, gram)
    arrive(7, gram.at[pl.ds(0, m - 1)])
    gram_ref[...] = gram[...].reshape(m * rows, m * rows)

    for phase, ref in ((0, a_src), (1, b_src), (2, c_src), (3, d_src), (5, g_src), (6, g_dst)):
        pltpu.make_async_copy(ref, ref, send.at[phase]).wait()
    for phase, ref in ((4, full), (7, gram)):
        sent = ref.at[pl.ds(0, m - 1)]
        pltpu.make_async_copy(sent, sent, send.at[phase]).wait()


def sketch_and_gram(omega, flexibility, block_row, block_sign):
    n, m = lax.axis_size("sub"), lax.axis_size("col")
    rows, width = omega.shape
    dofs = flexibility.shape[0]
    order = m * rows
    vmem = pl.BlockSpec(memory_space=pltpu.VMEM)
    return pl.pallas_call(
        functools.partial(sketch_kernel, n, m),
        out_shape=(
            jax.ShapeDtypeStruct((order, width), F32),
            jax.ShapeDtypeStruct((order, order), F32),
        ),
        in_specs=[vmem, pl.BlockSpec(memory_space=pl.ANY), vmem, vmem],
        out_specs=(vmem, vmem),
        scratch_shapes=[
            pltpu.VMEM((8, 1, dofs), F32),
            pltpu.VMEM((dofs, dofs), BF16),
            pltpu.VMEM((rows, width), F32),
            pltpu.VMEM((n, width), F32),
            pltpu.VMEM((n, dofs), F32),
            pltpu.VMEM((rows, dofs), F32),
            pltpu.VMEM((rows, dofs), F32),
            pltpu.VMEM((n, dofs), F32),
            pltpu.VMEM((n, width), F32),
            pltpu.VMEM((m, rows, width), F32),
            pltpu.VMEM((rows, order), F32),
            pltpu.VMEM((n, order), F32),
            pltpu.VMEM((1, order), F32),
            pltpu.VMEM((m, rows, order), F32),
            pltpu.SemaphoreType.DMA,
            pltpu.SemaphoreType.DMA((8,)),
            pltpu.SemaphoreType.DMA((8,)),
        ],
        compiler_params=pltpu.CompilerParams(collective_id=0, has_side_effects=True),
        name="sketch_and_gram",
    )(omega, flexibility, block_row.T, block_sign.T)


def shards(flexibility, omega, block_row, block_sign):
    full, gram = sketch_and_gram(omega, flexibility[0], block_row, block_sign)
    return finish(full, gram, omega.shape[0])


def solution(mesh):
    placed = (P("sub", None, None), P("col", "sub"), P(), P())
    return jax.shard_map(
        shards,
        mesh=mesh,
        in_specs=placed,
        out_specs=(P("col", "sub"), P("col", "sub"), P()),
        check_vma=False,
    )
```

```python
import functools

import jax
import jax.numpy as jnp
from jax import lax
from jax.experimental import pallas as pl
from jax.experimental.pallas import tpu as pltpu
from jax.sharding import PartitionSpec as P

F32 = jnp.float32
BF16 = jnp.bfloat16
NN = (((1,), (0,)), ((), ()))
NT = (((1,), (1,)), ((), ()))


def mm1(a, b, dims=NN):
    return lax.dot_general(a.astype(BF16), b.astype(BF16), dims, preferred_element_type=F32)


def halves(a):
    high = a.astype(BF16)
    return high, (a - high.astype(F32)).astype(BF16)


def mm3(a, b, dims=NN):
    ah, al = halves(a)
    bh, bl = halves(b)
    dot = functools.partial(lax.dot_general, dimension_numbers=dims, preferred_element_type=F32)
    return dot(ah, bh) + (dot(ah, bl) + dot(al, bh))


def finish_kernel(full_ref, gram_ref, sketch_ref, basis_ref, upper_ref, work, lower):
    order = gram_ref.shape[0]
    rows = basis_ref.shape[0]
    i_row = lax.broadcasted_iota(jnp.int32, (order, order), 0)
    i_col = lax.broadcasted_iota(jnp.int32, (order, order), 1)
    eye = jnp.where(i_row == i_col, 1.0, 0.0).astype(F32)
    phi_mask = jnp.where(i_row > i_col, 1.0, 0.5 * eye).astype(F32)
    gram = gram_ref[...]
    on_diag = gram * eye
    d_row = jnp.sum(on_diag, axis=0, keepdims=True)
    d_col = jnp.sum(on_diag, axis=1, keepdims=True)
    s_row = lax.rsqrt(d_row)
    s_col = lax.rsqrt(d_col)
    err = jnp.where(i_row == i_col, 0.0, gram * s_row * s_col)
    p = err * phi_mask
    n = mm1(p, p, NT) * phi_mask + mm1(p, p) - p
    z = err + n + mm1(n, err)
    resid = z + n.T + mm1(z, n, NT)
    p = resid * phi_mask
    n = n - p - mm1(p, n)
    z = err + n + mm3(n, err)
    resid = z + n.T + mm3(z, n, NT)
    p = resid * phi_mask
    n = n - p - mm1(p, n)
    miss = jnp.sum(resid * resid)
    z = err + n + mm3(n, err)
    upper_ref[...] = jnp.where(i_row <= i_col, (eye + z) * (d_row * s_row), 0.0)
    lower[...] = jnp.where(i_row >= i_col, (eye + n) * s_row, 0.0)

    @pl.when(jnp.logical_not(miss < 4e-6))
    def eliminate():
        work[...] = gram
        lower[...] = eye
        lane = lax.broadcasted_iota(jnp.int32, (1, order), 1)
        sub = lax.broadcasted_iota(jnp.int32, (order, 1), 0)

        @pl.loop(0, order)
        def step(j):
            remain = work[...]
            row = work[pl.ds(j, 1), :]
            pivot = jnp.sum(jnp.where(lane == j, row, 0.0), axis=1, keepdims=True)
            scale = 1.0 / jnp.sqrt(pivot)
            u_row = jnp.where(lane >= j, row * scale, 0.0)
            column = jnp.sum(jnp.where(i_col == j, remain, 0.0), axis=1, keepdims=True)
            column = jnp.where(sub > j, column * scale, 0.0)
            l_row = lower[pl.ds(j, 1), :] * scale
            upper_ref[pl.ds(j, 1), :] = u_row
            work[...] = remain - column * u_row
            below = lower[...] - column * l_row
            lower[...] = jnp.where(sub == j, l_row, below)

    mine = pl.ds(pl.multiple_of(lax.axis_index("col") * rows, rows), rows)
    basis_ref[...] = mm3(lower[mine, :], full_ref[...])
    sketch_ref[...] = full_ref[mine, :]


def finish(full, gram, rows):
    order, width = full.shape
    return pl.pallas_call(
        finish_kernel,
        out_shape=(
            jax.ShapeDtypeStruct((rows, width), F32),
            jax.ShapeDtypeStruct((rows, width), F32),
            jax.ShapeDtypeStruct((order, order), F32),
        ),
        in_specs=[pl.BlockSpec(memory_space=pltpu.VMEM)] * 2,
        out_specs=(pl.BlockSpec(memory_space=pltpu.VMEM),) * 3,
        scratch_shapes=[pltpu.VMEM((order, order), F32)] * 2,
        name="factor_and_basis",
    )(full, gram)


MESH = pl.DeviceIdType.MESH
RING = 8
PAIR = 2
TN = (((0,), (0,)), ((), ()))


def stack_lanes(x, length):
    return jnp.concatenate([x[:, k : k + length] for k in range(0, x.shape[1], length)], axis=0)


def spread_rows(x, parts):
    length = x.shape[0] // parts
    return jnp.concatenate([x[k * length : (k + 1) * length] for k in range(parts)], axis=1)


def centre_out(i, size):
    half = lax.div(i + 1, 2)
    return size // 2 + half * (1 - 2 * lax.rem(i, 2))


def sketch_kernel(
    n, m, omega_ref, flex_ref, row_ref, sign_ref, full_ref, gram_ref,
    spare, flex, a_src, a_dst, b_src, b_dst, c_src, c_dst, d_src, full, g_src, g_dst, h_src, h_dst, i_src, gram,
    flex_sem, send, recv,
):
    me = lax.axis_index("sub")
    col = lax.axis_index("col")
    rows, width = a_src.shape
    refs = row_ref.shape[0]
    length = b_src.shape[1] // refs
    owned = width // length

    load = pltpu.make_async_copy(flex_ref, flex, flex_sem)
    load.start()

    across = n // (RING * PAIR)
    plane = across * PAIR
    my_x = lax.div(me, RING * PAIR)
    my_z = lax.rem(lax.div(me, PAIR), RING)
    my_core = lax.rem(me, PAIR)
    my_part = my_x * PAIR + my_core

    def at(x, z, core):
        x, z, core = lax.rem(x, across), lax.rem(z, RING), lax.rem(core, PAIR)
        return (x * RING + z) * PAIR + core

    def peer_of(k):
        in_plane = lax.rem(k, plane)
        dz = centre_out(lax.div(k, plane), RING)
        dx = centre_out(lax.div(in_plane, PAIR), across)
        return at(my_x + dx, my_z + dz, my_core + 1 - lax.rem(in_plane, PAIR))

    plane_mates = [
        (dy, dx, core)
        for dy in (2, 1, 3, 0)
        for dx in (2, 1, 3, 0)
        for core in (1, 0)
        if (dy, dx, core) != (0, 0, 0)
    ]
    barrier = pltpu.get_barrier_semaphore()

    def greet(k, carry):
        pl.semaphore_signal(
            barrier, inc=1, device_id={"sub": peer_of(k)}, device_id_type=MESH
        )
        return carry

    lax.fori_loop(0, n - 1, greet, 0)
    others = [mate for mate in plane_mates if mate[0]]
    for dy, dx, core in others:
        pl.semaphore_signal(
            barrier, inc=1, device_id_type=MESH,
            device_id={"sub": at(my_x + dx, my_z, my_core + core), "col": lax.rem(col + dy, m)},
        )
    a_src[...] = omega_ref[...].astype(F32)
    pl.semaphore_wait(barrier, n - 1 + len(others))

    def start(phase, source, target):
        own = pltpu.make_async_copy(source(me), target, recv.at[phase])
        own.start()
        pltpu.make_async_copy(
            source(me), spare.at[phase, :, pl.ds(0, target.shape[1])], send.at[phase]
        ).start()

        def put(k, carry):
            peer = peer_of(k)
            pltpu.make_async_remote_copy(
                src_ref=source(peer), dst_ref=target, send_sem=send.at[phase],
                recv_sem=recv.at[phase], device_id={"sub": peer}, device_id_type=MESH,
            ).start()
            return carry

        lax.fori_loop(0, n - 1, put, 0)

    def arrive(phase, whole):
        pltpu.make_async_copy(whole, whole, recv.at[phase]).wait()

    def start_col(phase, ref):
        for k in range(1, m):
            pltpu.make_async_remote_copy(
                src_ref=ref.at[col], dst_ref=ref.at[col], send_sem=send.at[phase],
                recv_sem=recv.at[phase], device_id={"col": lax.rem(col + k, m)},
                device_id_type=MESH,
            ).start()

    def row_of(ref):
        return lambda r: ref.at[pl.ds(r, 1), :]

    start(0, row_of(a_src), a_dst.at[pl.ds(me, 1), :])
    spot = lax.broadcasted_iota(jnp.int32, (owned * n, n), 0)
    piece = sum([jnp.where(spot >= n * j, 1, 0) for j in range(1, owned)])
    named = owned * (spot - n * piece) + piece
    pick = jnp.concatenate(
        [
            jnp.where(row_ref[l : l + 1, :] == named, sign_ref[l : l + 1, :], 0).astype(F32)
            for l in range(refs)
        ],
        axis=1,
    ).astype(BF16)
    arrive(0, a_dst)
    wanted = lax.dot_general(
        pick, stack_lanes(a_dst[...], length).astype(BF16), TN, preferred_element_type=F32
    )
    b_src[...] = spread_rows(wanted, refs)

    start(1, row_of(b_src), b_dst.at[pl.ds(me, 1), :])
    load.wait()
    arrive(1, b_dst)
    c_src[...] = lax.dot_general(
        b_dst[...].astype(BF16), flex[...], NT, preferred_element_type=F32
    )

    start(2, row_of(c_src), c_dst.at[pl.ds(me, 1), :])
    arrive(2, c_dst)
    terms = stack_lanes(c_dst[...], length)
    high, rest = halves(terms)
    middle, low = halves(terms - high.astype(F32))
    total = sum(
        [lax.dot_general(pick, t, NN, preferred_element_type=F32) for t in (low, middle, high)]
    )
    d_src[...] = spread_rows(total, owned)

    start(3, row_of(d_src), full.at[col, pl.ds(me, 1), :])
    arrive(3, full.at[col])
    start_col(4, full)
    arrive(4, full.at[pl.ds(0, m - 1)])
    whole = full[...].reshape(m * rows, width)
    full_ref[...] = whole
    g_src[...] = mm3(full[col], whole, NT)

    group = rows // plane
    pltpu.make_async_copy(
        g_src.at[pl.ds(my_part * group, group), :], g_dst.at[my_part], recv.at[5]
    ).start()
    for _, dx, core in plane_mates[-(plane - 1) :]:
        part = lax.rem(my_x + dx, across) * PAIR + lax.rem(my_core + core, PAIR)
        pltpu.make_async_remote_copy(
            src_ref=g_src.at[pl.ds(part * group, group), :], dst_ref=g_dst.at[my_part],
            send_sem=send.at[5], recv_sem=recv.at[5], device_id_type=MESH,
            device_id={"sub": at(my_x + dx, my_z, my_core + core)},
        ).start()
    arrive(5, g_dst)
    h_src[...] = jnp.sum(g_dst[...], axis=0)

    pltpu.make_async_copy(h_src, h_dst.at[my_z], recv.at[6]).start()
    for dz in (4, 3, 5, 2, 6, 1, 7):
        pltpu.make_async_remote_copy(
            src_ref=h_src, dst_ref=h_dst.at[my_z], send_sem=send.at[6], recv_sem=recv.at[6],
            device_id={"sub": at(my_x, my_z + dz, my_core)}, device_id_type=MESH,
        ).start()
    arrive(6, h_dst)
    i_src[...] = jnp.sum(h_dst[...], axis=0) / (width * n)

    place = gram.at[col * plane + my_part]
    pltpu.make_async_copy(i_src, place, recv.at[7]).start()
    for dy, dx, core in plane_mates:
        pltpu.make_async_remote_copy(
            src_ref=i_src, dst_ref=place, send_sem=send.at[7], recv_sem=recv.at[7],
            device_id={"sub": at(my_x + dx, my_z, my_core + core), "col": lax.rem(col + dy, m)},
            device_id_type=MESH,
        ).start()
    arrive(7, gram)
    gram_ref[...] = gram[...].reshape(m * rows, m * rows)

    for phase, sent in (
        (0, a_src), (1, b_src), (2, c_src), (3, d_src), (4, full.at[pl.ds(0, m - 1)]),
        (5, g_dst.at[pl.ds(0, plane - 1)]), (6, h_dst.at[pl.ds(0, RING - 1)]),
        (7, gram.at[pl.ds(0, m * plane - 1)]),
    ):
        pltpu.make_async_copy(sent, sent, send.at[phase]).wait()


def sketch_and_gram(omega, flexibility, block_row, block_sign):
    n, m = lax.axis_size("sub"), lax.axis_size("col")
    rows, width = omega.shape
    dofs = flexibility.shape[0]
    order = m * rows
    plane = n // RING
    group = rows // plane
    vmem = pl.BlockSpec(memory_space=pltpu.VMEM)
    return pl.pallas_call(
        functools.partial(sketch_kernel, n, m),
        out_shape=(
            jax.ShapeDtypeStruct((order, width), F32),
            jax.ShapeDtypeStruct((order, order), F32),
        ),
        in_specs=[vmem, pl.BlockSpec(memory_space=pl.ANY), vmem, vmem],
        out_specs=(vmem, vmem),
        scratch_shapes=[
            pltpu.VMEM((8, 1, dofs), F32),
            pltpu.VMEM((dofs, dofs), BF16),
            pltpu.VMEM((rows, width), F32),
            pltpu.VMEM((n, width), F32),
            pltpu.VMEM((n, dofs), F32),
            pltpu.VMEM((rows, dofs), F32),
            pltpu.VMEM((rows, dofs), F32),
            pltpu.VMEM((n, dofs), F32),
            pltpu.VMEM((n, width), F32),
            pltpu.VMEM((m, rows, width), F32),
            pltpu.VMEM((rows, order), F32),
            pltpu.VMEM((plane, group, order), F32),
            pltpu.VMEM((group, order), F32),
            pltpu.VMEM((RING, group, order), F32),
            pltpu.VMEM((group, order), F32),
            pltpu.VMEM((m * plane, group, order), F32),
            pltpu.SemaphoreType.DMA,
            pltpu.SemaphoreType.DMA((8,)),
            pltpu.SemaphoreType.DMA((8,)),
        ],
        compiler_params=pltpu.CompilerParams(collective_id=0, has_side_effects=True),
        name="sketch_and_gram",
    )(omega, flexibility, block_row.T, block_sign.T)


def shards(flexibility, omega, block_row, block_sign):
    full, gram = sketch_and_gram(omega, flexibility[0], block_row, block_sign)
    return finish(full, gram, omega.shape[0])


def solution(mesh):
    placed = (P("sub", None, None), P("col", "sub"), P(), P())
    return jax.shard_map(
        shards,
        mesh=mesh,
        in_specs=placed,
        out_specs=(P("col", "sub"), P("col", "sub"), P()),
        check_vma=False,
    )
```

```python
import functools

import jax
import jax.numpy as jnp
from jax import lax
from jax.experimental import pallas as pl
from jax.experimental.pallas import tpu as pltpu
from jax.sharding import PartitionSpec as P

F32 = jnp.float32
BF16 = jnp.bfloat16
NN = (((1,), (0,)), ((), ()))
NT = (((1,), (1,)), ((), ()))


def mm1(a, b, dims=NN):
    return lax.dot_general(a.astype(BF16), b.astype(BF16), dims, preferred_element_type=F32)


def halves(a):
    high = a.astype(BF16)
    return high, (a - high.astype(F32)).astype(BF16)


def mm3(a, b, dims=NN):
    ah, al = halves(a)
    bh, bl = halves(b)
    dot = functools.partial(lax.dot_general, dimension_numbers=dims, preferred_element_type=F32)
    return dot(ah, bh) + (dot(ah, bl) + dot(al, bh))


def finish_kernel(full_ref, gram_ref, sketch_ref, basis_ref, upper_ref, work, lower):
    order = gram_ref.shape[0]
    rows = basis_ref.shape[0]
    i_row = lax.broadcasted_iota(jnp.int32, (order, order), 0)
    i_col = lax.broadcasted_iota(jnp.int32, (order, order), 1)
    eye = jnp.where(i_row == i_col, 1.0, 0.0).astype(F32)
    phi_mask = jnp.where(i_row > i_col, 1.0, 0.5 * eye).astype(F32)
    gram = gram_ref[...]
    on_diag = gram * eye
    d_row = jnp.sum(on_diag, axis=0, keepdims=True)
    d_col = jnp.sum(on_diag, axis=1, keepdims=True)
    s_row = lax.rsqrt(d_row)
    s_col = lax.rsqrt(d_col)
    err = jnp.where(i_row == i_col, 0.0, gram * s_row * s_col)
    p = err * phi_mask
    n = mm1(p, p, NT) * phi_mask + mm1(p, p) - p
    z = err + n + mm1(n, err)
    resid = z + n.T + mm1(z, n, NT)
    p = resid * phi_mask
    n = n - p - mm1(p, n)
    z = err + n + mm3(n, err)
    resid = z + n.T + mm3(z, n, NT)
    p = resid * phi_mask
    n = n - p - mm1(p, n)
    miss = jnp.sum(resid * resid)
    z = err + n + mm3(n, err)
    upper_ref[...] = jnp.where(i_row <= i_col, (eye + z) * (d_row * s_row), 0.0)
    lower[...] = jnp.where(i_row >= i_col, (eye + n) * s_row, 0.0)

    @pl.when(jnp.logical_not(miss < 4e-6))
    def eliminate():
        work[...] = gram
        lower[...] = eye
        lane = lax.broadcasted_iota(jnp.int32, (1, order), 1)
        sub = lax.broadcasted_iota(jnp.int32, (order, 1), 0)

        @pl.loop(0, order)
        def step(j):
            remain = work[...]
            row = work[pl.ds(j, 1), :]
            pivot = jnp.sum(jnp.where(lane == j, row, 0.0), axis=1, keepdims=True)
            scale = 1.0 / jnp.sqrt(pivot)
            u_row = jnp.where(lane >= j, row * scale, 0.0)
            column = jnp.sum(jnp.where(i_col == j, remain, 0.0), axis=1, keepdims=True)
            column = jnp.where(sub > j, column * scale, 0.0)
            l_row = lower[pl.ds(j, 1), :] * scale
            upper_ref[pl.ds(j, 1), :] = u_row
            work[...] = remain - column * u_row
            below = lower[...] - column * l_row
            lower[...] = jnp.where(sub == j, l_row, below)

    mine = pl.ds(pl.multiple_of(lax.axis_index("col") * rows, rows), rows)
    basis_ref[...] = mm3(lower[mine, :], full_ref[...])
    sketch_ref[...] = full_ref[mine, :]


def finish(full, gram, rows):
    order, width = full.shape
    return pl.pallas_call(
        finish_kernel,
        out_shape=(
            jax.ShapeDtypeStruct((rows, width), F32),
            jax.ShapeDtypeStruct((rows, width), F32),
            jax.ShapeDtypeStruct((order, order), F32),
        ),
        in_specs=[pl.BlockSpec(memory_space=pltpu.VMEM)] * 2,
        out_specs=(pl.BlockSpec(memory_space=pltpu.VMEM),) * 3,
        scratch_shapes=[pltpu.VMEM((order, order), F32)] * 2,
        compiler_params=pltpu.CompilerParams(vmem_limit_bytes=12 << 20),
        name="factor_and_basis",
    )(full, gram)


MESH = pl.DeviceIdType.MESH
RING = 8
PAIR = 2
TN = (((0,), (0,)), ((), ()))


def stack_lanes(x, length):
    return jnp.concatenate([x[:, k : k + length] for k in range(0, x.shape[1], length)], axis=0)


def spread_rows(x, parts):
    length = x.shape[0] // parts
    return jnp.concatenate([x[k * length : (k + 1) * length] for k in range(parts)], axis=1)


def centre_out(i, size):
    half = lax.div(i + 1, 2)
    return size // 2 + half * (1 - 2 * lax.rem(i, 2))


def sketch_kernel(
    n, m, omega_hbm, flex_ref, row_hbm, sign_hbm, full_ref, gram_ref,
    omega_ref, row_ref, sign_ref, load_sem, spare, flex, a_src, a_dst, b_src, b_dst, c_src, c_dst, d_src, full, g_src, g_dst, h_src, h_dst, i_src, gram,
    flex_sem, send, recv,
):
    me = lax.axis_index("sub")
    col = lax.axis_index("col")
    rows, width = a_src.shape
    refs = row_ref.shape[0]
    length = b_src.shape[1] // refs
    owned = width // length

    across = n // (RING * PAIR)
    plane = across * PAIR
    my_x = lax.div(me, RING * PAIR)
    my_z = lax.rem(lax.div(me, PAIR), RING)
    my_core = lax.rem(me, PAIR)
    my_part = my_x * PAIR + my_core

    def at(x, z, core):
        x, z, core = lax.rem(x, across), lax.rem(z, RING), lax.rem(core, PAIR)
        return (x * RING + z) * PAIR + core

    def peer_of(k):
        in_plane = lax.rem(k, plane)
        dz = centre_out(lax.div(k, plane), RING)
        dx = centre_out(lax.div(in_plane, PAIR), across)
        return at(my_x + dx, my_z + dz, my_core + 1 - lax.rem(in_plane, PAIR))

    plane_mates = [
        (dy, dx, core)
        for dy in (2, 1, 3, 0)
        for dx in (2, 1, 3, 0)
        for core in (1, 0)
        if (dy, dx, core) != (0, 0, 0)
    ]
    barrier = pltpu.get_barrier_semaphore()

    def greet(k, carry):
        pl.semaphore_signal(
            barrier, inc=1, device_id={"sub": peer_of(k)}, device_id_type=MESH
        )
        return carry

    lax.fori_loop(0, n - 1, greet, 0)
    others = [mate for mate in plane_mates if mate[0]]
    for dy, dx, core in others:
        pl.semaphore_signal(
            barrier, inc=1, device_id_type=MESH,
            device_id={"sub": at(my_x + dx, my_z, my_core + core), "col": lax.rem(col + dy, m)},
        )
    tables = [
        pltpu.make_async_copy(row_hbm, row_ref, load_sem.at[1]),
        pltpu.make_async_copy(sign_hbm, sign_ref, load_sem.at[2]),
    ]
    load = pltpu.make_async_copy(flex_ref, flex, flex_sem)
    first = pltpu.make_async_copy(omega_hbm, omega_ref, load_sem.at[0])
    for copy in [first, *tables, load]:
        copy.start()
    first.wait()
    a_src[...] = omega_ref[...].astype(F32)
    pl.semaphore_wait(barrier, n - 1 + len(others))

    def start(phase, source, target):
        own = pltpu.make_async_copy(source(me), target, recv.at[phase])
        own.start()
        pltpu.make_async_copy(
            source(me), spare.at[phase, :, pl.ds(0, target.shape[1])], send.at[phase]
        ).start()

        def put(k, carry):
            peer = peer_of(k)
            pltpu.make_async_remote_copy(
                src_ref=source(peer), dst_ref=target, send_sem=send.at[phase],
                recv_sem=recv.at[phase], device_id={"sub": peer}, device_id_type=MESH,
            ).start()
            return carry

        lax.fori_loop(0, n - 1, put, 0)

    def arrive(phase, whole):
        pltpu.make_async_copy(whole, whole, recv.at[phase]).wait()

    def start_col(phase, ref):
        for k in range(1, m):
            pltpu.make_async_remote_copy(
                src_ref=ref.at[col], dst_ref=ref.at[col], send_sem=send.at[phase],
                recv_sem=recv.at[phase], device_id={"col": lax.rem(col + k, m)},
                device_id_type=MESH,
            ).start()

    def row_of(ref):
        return lambda r: ref.at[pl.ds(r, 1), :]

    start(0, row_of(a_src), a_dst.at[pl.ds(me, 1), :])
    for copy in tables:
        copy.wait()
    spot = lax.broadcasted_iota(jnp.int32, (owned * n, n), 0)
    piece = sum([jnp.where(spot >= n * j, 1, 0) for j in range(1, owned)])
    named = owned * (spot - n * piece) + piece
    pick = jnp.concatenate(
        [
            jnp.where(row_ref[l : l + 1, :] == named, sign_ref[l : l + 1, :], 0).astype(F32)
            for l in range(refs)
        ],
        axis=1,
    ).astype(BF16)
    arrive(0, a_dst)
    wanted = lax.dot_general(
        pick, stack_lanes(a_dst[...], length).astype(BF16), TN, preferred_element_type=F32
    )
    b_src[...] = spread_rows(wanted, refs)

    start(1, row_of(b_src), b_dst.at[pl.ds(me, 1), :])
    load.wait()
    arrive(1, b_dst)
    c_src[...] = lax.dot_general(
        b_dst[...].astype(BF16), flex[...], NT, preferred_element_type=F32
    )

    start(2, row_of(c_src), c_dst.at[pl.ds(me, 1), :])
    arrive(2, c_dst)
    terms = stack_lanes(c_dst[...], length)
    high, rest = halves(terms)
    middle, low = halves(terms - high.astype(F32))
    total = sum(
        [lax.dot_general(pick, t, NN, preferred_element_type=F32) for t in (low, middle, high)]
    )
    d_src[...] = spread_rows(total, owned)

    start(3, row_of(d_src), full.at[col, pl.ds(me, 1), :])
    arrive(3, full.at[col])
    start_col(4, full)
    arrive(4, full.at[pl.ds(0, m - 1)])
    whole = full[...].reshape(m * rows, width)
    full_ref[...] = whole
    g_src[...] = mm3(full[col], whole, NT)

    group = rows // plane
    pltpu.make_async_copy(
        g_src.at[pl.ds(my_part * group, group), :], g_dst.at[my_part], recv.at[5]
    ).start()
    for _, dx, core in plane_mates[-(plane - 1) :]:
        part = lax.rem(my_x + dx, across) * PAIR + lax.rem(my_core + core, PAIR)
        pltpu.make_async_remote_copy(
            src_ref=g_src.at[pl.ds(part * group, group), :], dst_ref=g_dst.at[my_part],
            send_sem=send.at[5], recv_sem=recv.at[5], device_id_type=MESH,
            device_id={"sub": at(my_x + dx, my_z, my_core + core)},
        ).start()
    arrive(5, g_dst)
    h_src[...] = jnp.sum(g_dst[...], axis=0)

    pltpu.make_async_copy(h_src, h_dst.at[my_z], recv.at[6]).start()
    for dz in (4, 3, 5, 2, 6, 1, 7):
        pltpu.make_async_remote_copy(
            src_ref=h_src, dst_ref=h_dst.at[my_z], send_sem=send.at[6], recv_sem=recv.at[6],
            device_id={"sub": at(my_x, my_z + dz, my_core)}, device_id_type=MESH,
        ).start()
    arrive(6, h_dst)
    i_src[...] = jnp.sum(h_dst[...], axis=0) / (width * n)

    place = gram.at[col * plane + my_part]
    pltpu.make_async_copy(i_src, place, recv.at[7]).start()
    for dy, dx, core in plane_mates:
        pltpu.make_async_remote_copy(
            src_ref=i_src, dst_ref=place, send_sem=send.at[7], recv_sem=recv.at[7],
            device_id={"sub": at(my_x + dx, my_z, my_core + core), "col": lax.rem(col + dy, m)},
            device_id_type=MESH,
        ).start()
    arrive(7, gram)
    gram_ref[...] = gram[...].reshape(m * rows, m * rows)

    for phase, sent in (
        (0, a_src), (1, b_src), (2, c_src), (3, d_src), (4, full.at[pl.ds(0, m - 1)]),
        (5, g_dst.at[pl.ds(0, plane - 1)]), (6, h_dst.at[pl.ds(0, RING - 1)]),
        (7, gram.at[pl.ds(0, m * plane - 1)]),
    ):
        pltpu.make_async_copy(sent, sent, send.at[phase]).wait()


def sketch_and_gram(omega, flexibility, block_row, block_sign):
    n, m = lax.axis_size("sub"), lax.axis_size("col")
    rows, width = omega.shape
    dofs = flexibility.shape[0]
    order = m * rows
    plane = n // RING
    group = rows // plane
    vmem = pl.BlockSpec(memory_space=pltpu.VMEM)
    return pl.pallas_call(
        functools.partial(sketch_kernel, n, m),
        out_shape=(
            jax.ShapeDtypeStruct((order, width), F32),
            jax.ShapeDtypeStruct((order, order), F32),
        ),
        in_specs=[pl.BlockSpec(memory_space=pltpu.HBM)] * 4,
        out_specs=(vmem, vmem),
        scratch_shapes=[
            pltpu.VMEM(omega.shape, omega.dtype),
            pltpu.VMEM(block_row.shape[::-1], jnp.int32),
            pltpu.VMEM(block_row.shape[::-1], jnp.int32),
            pltpu.SemaphoreType.DMA((3,)),
            pltpu.VMEM((8, 1, dofs), F32),
            pltpu.VMEM((dofs, dofs), BF16),
            pltpu.VMEM((rows, width), F32),
            pltpu.VMEM((n, width), F32),
            pltpu.VMEM((n, dofs), F32),
            pltpu.VMEM((rows, dofs), F32),
            pltpu.VMEM((rows, dofs), F32),
            pltpu.VMEM((n, dofs), F32),
            pltpu.VMEM((n, width), F32),
            pltpu.VMEM((m, rows, width), F32),
            pltpu.VMEM((rows, order), F32),
            pltpu.VMEM((plane, group, order), F32),
            pltpu.VMEM((group, order), F32),
            pltpu.VMEM((RING, group, order), F32),
            pltpu.VMEM((group, order), F32),
            pltpu.VMEM((m * plane, group, order), F32),
            pltpu.SemaphoreType.DMA,
            pltpu.SemaphoreType.DMA((8,)),
            pltpu.SemaphoreType.DMA((8,)),
        ],
        compiler_params=pltpu.CompilerParams(
            collective_id=0, has_side_effects=True, vmem_limit_bytes=12 << 20
        ),
        name="sketch_and_gram",
    )(omega, flexibility, block_row.T, block_sign.T)


def shards(flexibility, omega, block_row, block_sign):
    full, gram = sketch_and_gram(omega, flexibility[0], block_row, block_sign)
    return finish(full, gram, omega.shape[0])


def solution(mesh):
    placed = (P("sub", None, None), P("col", "sub"), P(), P())
    return jax.shard_map(
        shards,
        mesh=mesh,
        in_specs=placed,
        out_specs=(P("col", "sub"), P("col", "sub"), P()),
        check_vma=False,
    )
```

```python
import functools

import jax
import jax.numpy as jnp
from jax import lax
from jax.experimental import pallas as pl
from jax.experimental.pallas import tpu as pltpu
from jax.sharding import PartitionSpec as P

F32 = jnp.float32
BF16 = jnp.bfloat16
NN = (((1,), (0,)), ((), ()))
NT = (((1,), (1,)), ((), ()))


def mm1(a, b, dims=NN):
    return lax.dot_general(a.astype(BF16), b.astype(BF16), dims, preferred_element_type=F32)


def halves(a):
    high = a.astype(BF16)
    return high, (a - high.astype(F32)).astype(BF16)


def mm3(a, b, dims=NN):
    ah, al = halves(a)
    bh, bl = halves(b)
    dot = functools.partial(lax.dot_general, dimension_numbers=dims, preferred_element_type=F32)
    return dot(ah, bh) + (dot(ah, bl) + dot(al, bh))


def finish_kernel(full_ref, gram_ref, sketch_ref, basis_ref, upper_ref, work, lower):
    order = gram_ref.shape[0]
    rows = basis_ref.shape[0]
    i_row = lax.broadcasted_iota(jnp.int32, (order, order), 0)
    i_col = lax.broadcasted_iota(jnp.int32, (order, order), 1)
    eye = jnp.where(i_row == i_col, 1.0, 0.0).astype(F32)
    phi_mask = jnp.where(i_row > i_col, 1.0, 0.5 * eye).astype(F32)
    gram = gram_ref[...]
    on_diag = gram * eye
    d_row = jnp.sum(on_diag, axis=0, keepdims=True)
    d_col = jnp.sum(on_diag, axis=1, keepdims=True)
    s_row = lax.rsqrt(d_row)
    s_col = lax.rsqrt(d_col)
    err = jnp.where(i_row == i_col, 0.0, gram * s_row * s_col)
    p = err * phi_mask
    n = mm1(p, p, NT) * phi_mask + mm1(p, p) - p
    z = err + n + mm1(n, err)
    resid = z + n.T + mm1(z, n, NT)
    p = resid * phi_mask
    n = n - p - mm1(p, n)
    z = err + n + mm3(n, err)
    resid = z + n.T + mm3(z, n, NT)
    p = resid * phi_mask
    n = n - p - mm1(p, n)
    miss = jnp.sum(resid * resid)
    z = err + n + mm3(n, err)
    upper_ref[...] = jnp.where(i_row <= i_col, (eye + z) * (d_row * s_row), 0.0)
    lower[...] = jnp.where(i_row >= i_col, (eye + n) * s_row, 0.0)

    @pl.when(jnp.logical_not(miss < 4e-6))
    def eliminate():
        work[...] = gram
        lower[...] = eye
        lane = lax.broadcasted_iota(jnp.int32, (1, order), 1)
        sub = lax.broadcasted_iota(jnp.int32, (order, 1), 0)

        @pl.loop(0, order)
        def step(j):
            remain = work[...]
            row = work[pl.ds(j, 1), :]
            pivot = jnp.sum(jnp.where(lane == j, row, 0.0), axis=1, keepdims=True)
            scale = 1.0 / jnp.sqrt(pivot)
            u_row = jnp.where(lane >= j, row * scale, 0.0)
            column = jnp.sum(jnp.where(i_col == j, remain, 0.0), axis=1, keepdims=True)
            column = jnp.where(sub > j, column * scale, 0.0)
            l_row = lower[pl.ds(j, 1), :] * scale
            upper_ref[pl.ds(j, 1), :] = u_row
            work[...] = remain - column * u_row
            below = lower[...] - column * l_row
            lower[...] = jnp.where(sub == j, l_row, below)

    mine = pl.ds(pl.multiple_of(lax.axis_index("col") * rows, rows), rows)
    basis_ref[...] = mm3(lower[mine, :], full_ref[...])
    sketch_ref[...] = full_ref[mine, :]


def finish(full, gram, rows):
    order, width = full.shape
    return pl.pallas_call(
        finish_kernel,
        out_shape=(
            jax.ShapeDtypeStruct((rows, width), F32),
            jax.ShapeDtypeStruct((rows, width), F32),
            jax.ShapeDtypeStruct((order, order), F32),
        ),
        in_specs=[pl.BlockSpec(memory_space=pltpu.VMEM)] * 2,
        out_specs=(pl.BlockSpec(memory_space=pltpu.VMEM),) * 3,
        scratch_shapes=[pltpu.VMEM((order, order), F32)] * 2,
        compiler_params=pltpu.CompilerParams(vmem_limit_bytes=12 << 20),
        name="factor_and_basis",
    )(full, gram)


MESH = pl.DeviceIdType.MESH
RING = 8
PAIR = 2
TN = (((0,), (0,)), ((), ()))


def stack_lanes(x, length):
    return jnp.concatenate([x[:, k : k + length] for k in range(0, x.shape[1], length)], axis=0)


def spread_rows(x, parts):
    length = x.shape[0] // parts
    return jnp.concatenate([x[k * length : (k + 1) * length] for k in range(parts)], axis=1)


def centre_out(i, size):
    half = lax.div(i + 1, 2)
    return size // 2 + half * (1 - 2 * lax.rem(i, 2))


def sketch_kernel(
    n, m, omega_hbm, flex_ref, row_hbm, sign_hbm, full_ref, gram_ref,
    omega_ref, row_ref, sign_ref, load_sem, spare, flex, a_src, a_dst, b_src, b_dst, c_src, c_dst, d_src, full, g_src, g_dst, h_src, h_dst, i_src, gram,
    flex_sem, send, recv,
):
    me = lax.axis_index("sub")
    col = lax.axis_index("col")
    rows, width = a_src.shape
    refs = row_ref.shape[0]
    length = b_src.shape[1] // refs
    owned = width // length

    across = n // (RING * PAIR)
    plane = across * PAIR
    my_x = lax.div(me, RING * PAIR)
    my_z = lax.rem(lax.div(me, PAIR), RING)
    my_core = lax.rem(me, PAIR)
    my_part = my_x * PAIR + my_core

    def at(x, z, core):
        x, z, core = lax.rem(x, across), lax.rem(z, RING), lax.rem(core, PAIR)
        return (x * RING + z) * PAIR + core

    def peer_of(k):
        in_plane = lax.rem(k, plane)
        dz = centre_out(lax.div(k, plane), RING)
        dx = centre_out(lax.div(in_plane, PAIR), across)
        return at(my_x + dx, my_z + dz, my_core + 1 - lax.rem(in_plane, PAIR))

    plane_mates = [
        (dy, dx, core)
        for dy in (2, 1, 3, 0)
        for dx in (2, 1, 3, 0)
        for core in (1, 0)
        if (dy, dx, core) != (0, 0, 0)
    ]
    barrier = pltpu.get_barrier_semaphore()

    def greet(k, carry):
        pl.semaphore_signal(
            barrier, inc=1, device_id={"sub": peer_of(k)}, device_id_type=MESH
        )
        return carry

    lax.fori_loop(0, n - 1, greet, 0)
    others = [mate for mate in plane_mates if mate[0]]
    for dy, dx, core in others:
        pl.semaphore_signal(
            barrier, inc=1, device_id_type=MESH,
            device_id={"sub": at(my_x + dx, my_z, my_core + core), "col": lax.rem(col + dy, m)},
        )
    tables = [
        pltpu.make_async_copy(row_hbm, row_ref, load_sem.at[1]),
        pltpu.make_async_copy(sign_hbm, sign_ref, load_sem.at[2]),
    ]
    load = pltpu.make_async_copy(flex_ref, flex, flex_sem)
    first = pltpu.make_async_copy(omega_hbm, omega_ref, load_sem.at[0])
    for copy in [first, *tables, load]:
        copy.start()
    first.wait()
    a_src[...] = omega_ref[...].astype(F32)
    pl.semaphore_wait(barrier, n - 1 + len(others))

    def start(phase, source, target):
        own = pltpu.make_async_copy(source(me), target, recv.at[phase])
        own.start()
        pltpu.make_async_copy(
            source(me), spare.at[phase, :, pl.ds(0, target.shape[1])], send.at[phase]
        ).start()

        def put(k, carry):
            peer = peer_of(k)
            pltpu.make_async_remote_copy(
                src_ref=source(peer), dst_ref=target, send_sem=send.at[phase],
                recv_sem=recv.at[phase], device_id={"sub": peer}, device_id_type=MESH,
            ).start()
            return carry

        lax.fori_loop(0, n - 1, put, 0)

    def arrive(phase, whole):
        pltpu.make_async_copy(whole, whole, recv.at[phase]).wait()

    def start_col(phase, ref):
        for k in range(1, m):
            pltpu.make_async_remote_copy(
                src_ref=ref.at[col], dst_ref=ref.at[col], send_sem=send.at[phase],
                recv_sem=recv.at[phase], device_id={"col": lax.rem(col + k, m)},
                device_id_type=MESH,
            ).start()

    def row_of(ref):
        return lambda r: ref.at[pl.ds(r, 1), :]

    start(0, row_of(a_src), a_dst.at[pl.ds(me, 1), :])
    for copy in tables:
        copy.wait()
    spot = lax.broadcasted_iota(jnp.int32, (owned * n, n), 0)
    piece = sum([jnp.where(spot >= n * j, 1, 0) for j in range(1, owned)])
    named = owned * (spot - n * piece) + piece
    pick = jnp.concatenate(
        [
            jnp.where(row_ref[l : l + 1, :] == named, sign_ref[l : l + 1, :], 0).astype(F32)
            for l in range(refs)
        ],
        axis=1,
    ).astype(BF16)
    arrive(0, a_dst)
    wanted = lax.dot_general(
        pick, stack_lanes(a_dst[...], length).astype(BF16), TN, preferred_element_type=F32
    )
    b_src[...] = spread_rows(wanted, refs)

    start(1, row_of(b_src), b_dst.at[pl.ds(me, 1), :])
    load.wait()
    arrive(1, b_dst)
    c_src[...] = lax.dot_general(
        b_dst[...].astype(BF16), flex[...], NT, preferred_element_type=F32
    )

    start(2, row_of(c_src), c_dst.at[pl.ds(me, 1), :])
    arrive(2, c_dst)
    terms = stack_lanes(c_dst[...], length)
    high, rest = halves(terms)
    middle, low = halves(terms - high.astype(F32))
    total = sum(
        [lax.dot_general(pick, t, NN, preferred_element_type=F32) for t in (low, middle, high)]
    )
    d_src[...] = spread_rows(total, owned)

    start(3, row_of(d_src), full.at[col, pl.ds(me, 1), :])
    arrive(3, full.at[col])
    start_col(4, full)
    arrive(4, full.at[pl.ds(0, m - 1)])
    whole = full[...].reshape(m * rows, width)
    full_ref[...] = whole
    g_src[...] = mm3(full[col], whole, NT)

    group = rows // plane
    pltpu.make_async_copy(
        g_src.at[pl.ds(my_part * group, group), :], g_dst.at[my_part], recv.at[5]
    ).start()
    for _, dx, core in plane_mates[-(plane - 1) :]:
        part = lax.rem(my_x + dx, across) * PAIR + lax.rem(my_core + core, PAIR)
        pltpu.make_async_remote_copy(
            src_ref=g_src.at[pl.ds(part * group, group), :], dst_ref=g_dst.at[my_part],
            send_sem=send.at[5], recv_sem=recv.at[5], device_id_type=MESH,
            device_id={"sub": at(my_x + dx, my_z, my_core + core)},
        ).start()
    arrive(5, g_dst)
    h_src[...] = jnp.sum(g_dst[...], axis=0)

    pltpu.make_async_copy(h_src, h_dst.at[my_z], recv.at[6]).start()
    for dz in (4, 3, 5, 2, 6, 1, 7):
        pltpu.make_async_remote_copy(
            src_ref=h_src, dst_ref=h_dst.at[my_z], send_sem=send.at[6], recv_sem=recv.at[6],
            device_id={"sub": at(my_x, my_z + dz, my_core)}, device_id_type=MESH,
        ).start()
    arrive(6, h_dst)
    i_src[...] = jnp.sum(h_dst[...], axis=0) / (width * n)

    place = gram.at[col * plane + my_part]
    pltpu.make_async_copy(i_src, place, recv.at[7]).start()
    for dy, dx, core in plane_mates:
        pltpu.make_async_remote_copy(
            src_ref=i_src, dst_ref=place, send_sem=send.at[7], recv_sem=recv.at[7],
            device_id={"sub": at(my_x + dx, my_z, my_core + core), "col": lax.rem(col + dy, m)},
            device_id_type=MESH,
        ).start()
    arrive(7, gram)
    gram_ref[...] = gram[...].reshape(m * rows, m * rows)

    for phase, sent in (
        (0, a_src), (1, b_src), (2, c_src), (3, d_src), (4, full.at[pl.ds(0, m - 1)]),
        (5, g_dst.at[pl.ds(0, plane - 1)]), (6, h_dst.at[pl.ds(0, RING - 1)]),
        (7, gram.at[pl.ds(0, m * plane - 1)]),
    ):
        pltpu.make_async_copy(sent, sent, send.at[phase]).wait()


def sketch_and_gram(omega, flexibility, block_row, block_sign):
    n, m = lax.axis_size("sub"), lax.axis_size("col")
    rows, width = omega.shape
    dofs = flexibility.shape[0]
    order = m * rows
    plane = n // RING
    group = rows // plane
    vmem = pl.BlockSpec(memory_space=pltpu.VMEM)
    return pl.pallas_call(
        functools.partial(sketch_kernel, n, m),
        out_shape=(
            jax.ShapeDtypeStruct((order, width), F32),
            jax.ShapeDtypeStruct((order, order), F32),
        ),
        in_specs=[pl.BlockSpec(memory_space=pltpu.HBM)] * 4,
        out_specs=(vmem, vmem),
        scratch_shapes=[
            pltpu.VMEM(omega.shape, omega.dtype),
            pltpu.VMEM(block_row.shape[::-1], jnp.int32),
            pltpu.VMEM(block_row.shape[::-1], jnp.int32),
            pltpu.SemaphoreType.DMA((3,)),
            pltpu.VMEM((8, 1, dofs), F32),
            pltpu.VMEM((dofs, dofs), BF16),
            pltpu.VMEM((rows, width), F32),
            pltpu.VMEM((n, width), F32),
            pltpu.VMEM((n, dofs), F32),
            pltpu.VMEM((rows, dofs), F32),
            pltpu.VMEM((rows, dofs), F32),
            pltpu.VMEM((n, dofs), F32),
            pltpu.VMEM((n, width), F32),
            pltpu.VMEM((m, rows, width), F32),
            pltpu.VMEM((rows, order), F32),
            pltpu.VMEM((plane, group, order), F32),
            pltpu.VMEM((group, order), F32),
            pltpu.VMEM((RING, group, order), F32),
            pltpu.VMEM((group, order), F32),
            pltpu.VMEM((m * plane, group, order), F32),
            pltpu.SemaphoreType.DMA,
            pltpu.SemaphoreType.DMA((8,)),
            pltpu.SemaphoreType.DMA((8,)),
        ],
        compiler_params=pltpu.CompilerParams(
            collective_id=0, has_side_effects=True, vmem_limit_bytes=12 << 20
        ),
        name="sketch_and_gram",
    )(*(pltpu.with_memory_space_constraint(x, pltpu.HBM) for x in (omega, flexibility, block_row.T, block_sign.T)))


def shards(flexibility, omega, block_row, block_sign):
    full, gram = sketch_and_gram(omega, flexibility[0], block_row, block_sign)
    return finish(full, gram, omega.shape[0])


def solution(mesh):
    placed = (P("sub", None, None), P("col", "sub"), P(), P())
    return jax.shard_map(
        shards,
        mesh=mesh,
        in_specs=placed,
        out_specs=(P("col", "sub"), P("col", "sub"), P()),
        check_vma=False,
    )
```

```python
import functools

import jax
import jax.numpy as jnp
from jax import lax
from jax.experimental import pallas as pl
from jax.experimental.pallas import tpu as pltpu
from jax.sharding import PartitionSpec as P

F32 = jnp.float32
BF16 = jnp.bfloat16
NN = (((1,), (0,)), ((), ()))
NT = (((1,), (1,)), ((), ()))


def mm1(a, b, dims=NN):
    return lax.dot_general(a.astype(BF16), b.astype(BF16), dims, preferred_element_type=F32)


def halves(a):
    high = a.astype(BF16)
    return high, (a - high.astype(F32)).astype(BF16)


def mm3(a, b, dims=NN):
    ah, al = halves(a)
    bh, bl = halves(b)
    dot = functools.partial(lax.dot_general, dimension_numbers=dims, preferred_element_type=F32)
    return dot(ah, bh) + (dot(ah, bl) + dot(al, bh))


def finish_kernel(full_ref, gram_ref, sketch_ref, basis_ref, upper_ref, work, lower):
    order = gram_ref.shape[0]
    rows = basis_ref.shape[0]
    i_row = lax.broadcasted_iota(jnp.int32, (order, order), 0)
    i_col = lax.broadcasted_iota(jnp.int32, (order, order), 1)
    eye = jnp.where(i_row == i_col, 1.0, 0.0).astype(F32)
    phi_mask = jnp.where(i_row > i_col, 1.0, 0.5 * eye).astype(F32)
    gram = gram_ref[...]
    on_diag = gram * eye
    d_row = jnp.sum(on_diag, axis=0, keepdims=True)
    d_col = jnp.sum(on_diag, axis=1, keepdims=True)
    s_row = lax.rsqrt(d_row)
    s_col = lax.rsqrt(d_col)
    err = jnp.where(i_row == i_col, 0.0, gram * s_row * s_col)
    p = err * phi_mask
    n = mm1(p, p, NT) * phi_mask + mm1(p, p) - p
    z = err + n + mm1(n, err)
    resid = z + n.T + mm1(z, n, NT)
    p = resid * phi_mask
    n = n - p - mm1(p, n)
    z = err + n + mm3(n, err)
    resid = z + n.T + mm3(z, n, NT)
    p = resid * phi_mask
    n = n - p - mm1(p, n)
    miss = jnp.sum(resid * resid)
    z = err + n + mm3(n, err)
    upper_ref[...] = jnp.where(i_row <= i_col, (eye + z) * (d_row * s_row), 0.0)
    lower[...] = jnp.where(i_row >= i_col, (eye + n) * s_row, 0.0)

    @pl.when(jnp.logical_not(miss < 4e-6))
    def eliminate():
        work[...] = gram
        lower[...] = eye
        lane = lax.broadcasted_iota(jnp.int32, (1, order), 1)
        sub = lax.broadcasted_iota(jnp.int32, (order, 1), 0)

        @pl.loop(0, order)
        def step(j):
            remain = work[...]
            row = work[pl.ds(j, 1), :]
            pivot = jnp.sum(jnp.where(lane == j, row, 0.0), axis=1, keepdims=True)
            scale = 1.0 / jnp.sqrt(pivot)
            u_row = jnp.where(lane >= j, row * scale, 0.0)
            column = jnp.sum(jnp.where(i_col == j, remain, 0.0), axis=1, keepdims=True)
            column = jnp.where(sub > j, column * scale, 0.0)
            l_row = lower[pl.ds(j, 1), :] * scale
            upper_ref[pl.ds(j, 1), :] = u_row
            work[...] = remain - column * u_row
            below = lower[...] - column * l_row
            lower[...] = jnp.where(sub == j, l_row, below)

    mine = pl.ds(pl.multiple_of(lax.axis_index("col") * rows, rows), rows)
    basis_ref[...] = mm3(lower[mine, :], full_ref[...])
    sketch_ref[...] = full_ref[mine, :]


def finish(full, gram, rows):
    order, width = full.shape
    return pl.pallas_call(
        finish_kernel,
        out_shape=(
            jax.ShapeDtypeStruct((rows, width), F32),
            jax.ShapeDtypeStruct((rows, width), F32),
            jax.ShapeDtypeStruct((order, order), F32),
        ),
        in_specs=[pl.BlockSpec(memory_space=pltpu.VMEM)] * 2,
        out_specs=(pl.BlockSpec(memory_space=pltpu.VMEM),) * 3,
        scratch_shapes=[pltpu.VMEM((order, order), F32)] * 2,
        compiler_params=pltpu.CompilerParams(vmem_limit_bytes=12 << 20),
        name="factor_and_basis",
    )(full, gram)


MESH = pl.DeviceIdType.MESH
RING = 8
PAIR = 2
TN = (((0,), (0,)), ((), ()))


def stack_lanes(x, length):
    return jnp.concatenate([x[:, k : k + length] for k in range(0, x.shape[1], length)], axis=0)


def spread_rows(x, parts):
    length = x.shape[0] // parts
    return jnp.concatenate([x[k * length : (k + 1) * length] for k in range(parts)], axis=1)


def centre_out(i, size):
    half = lax.div(i + 1, 2)
    return size // 2 + half * (1 - 2 * lax.rem(i, 2))


def sketch_kernel(
    n, m, omega_hbm, flex_ref, row_hbm, sign_hbm, full_ref, gram_ref,
    omega_ref, row_ref, sign_ref, load_sem, spare, flex, a_src, a_dst, b_src, b_dst, c_src, c_dst, d_src, full, g_src, g_dst, h_src, h_dst, i_src, gram,
    flex_sem, send, recv,
):
    me = lax.axis_index("sub")
    col = lax.axis_index("col")
    rows, width = a_src.shape
    refs = row_ref.shape[0]
    length = b_src.shape[1] // refs
    owned = width // length

    across = n // (RING * PAIR)
    plane = across * PAIR
    my_x = lax.div(me, RING * PAIR)
    my_z = lax.rem(lax.div(me, PAIR), RING)
    my_core = lax.rem(me, PAIR)
    my_part = my_x * PAIR + my_core

    def at(x, z, core):
        x, z, core = lax.rem(x, across), lax.rem(z, RING), lax.rem(core, PAIR)
        return (x * RING + z) * PAIR + core

    def offset_of(k):
        in_plane = lax.rem(k, plane)
        dz = centre_out(lax.div(k, plane), RING)
        dx = centre_out(lax.div(in_plane, PAIR), across)
        return dx, dz, 1 - lax.rem(in_plane, PAIR)

    def ahead(k):
        dx, dz, core = offset_of(k)
        return at(my_x + dx, my_z + dz, my_core + core)

    def behind(k):
        dx, dz, core = offset_of(k)
        return at(my_x + across - dx, my_z + RING - dz, my_core + core)

    def row_of(device):
        x = lax.div(device, RING * PAIR)
        z = lax.rem(lax.div(device, PAIR), RING)
        return z * plane + x * PAIR + lax.rem(device, PAIR)

    my_row = row_of(me)
    far = 3 * plane
    plane_mates = [
        (dy, dx, core)
        for dy in (2, 1, 3, 0)
        for dx in (2, 1, 3, 0)
        for core in (1, 0)
        if (dy, dx, core) != (0, 0, 0)
    ]
    barrier = pltpu.get_barrier_semaphore()

    def greet(k, carry):
        pl.semaphore_signal(
            barrier, inc=1, device_id={"sub": ahead(k)}, device_id_type=MESH
        )
        return carry

    lax.fori_loop(0, n - 1, greet, 0)
    others = [mate for mate in plane_mates if mate[0]]
    for dy, dx, core in others:
        pl.semaphore_signal(
            barrier, inc=1, device_id_type=MESH,
            device_id={"sub": at(my_x + dx, my_z, my_core + core), "col": lax.rem(col + dy, m)},
        )
    tables = [
        pltpu.make_async_copy(row_hbm, row_ref, load_sem.at[1]),
        pltpu.make_async_copy(sign_hbm, sign_ref, load_sem.at[2]),
    ]
    load = pltpu.make_async_copy(flex_ref, flex, flex_sem)
    first = pltpu.make_async_copy(omega_hbm, omega_ref, load_sem.at[0])
    for copy in [first, *tables, load]:
        copy.start()
    first.wait()
    a_src[...] = omega_ref[...].astype(F32)
    pl.semaphore_wait(barrier, n - 1 + len(others))

    def send_rows(phase, arrival, span, peer_of, source, target):
        def put(k, carry):
            peer = peer_of(k)
            pltpu.make_async_remote_copy(
                src_ref=source(k, peer), dst_ref=target(k), send_sem=send.at[phase],
                recv_sem=recv.at[arrival], device_id={"sub": peer}, device_id_type=MESH,
            ).start()
            return carry

        lax.fori_loop(*span, put, 0)

    def keep_row(phase, arrival, source, target):
        pltpu.make_async_copy(source, target, recv.at[arrival]).start()
        pltpu.make_async_copy(
            source, spare.at[phase, :, pl.ds(0, source.shape[1])], send.at[phase]
        ).start()

    def arrive(phase, whole):
        pltpu.make_async_copy(whole, whole, recv.at[phase]).wait()

    def row(ref, r):
        return ref.at[pl.ds(r, 1), :]

    send_rows(
        0, 0, (0, n - 1), ahead, lambda k, peer: row(a_src, row_of(peer)),
        lambda k: row(a_dst, me),
    )
    keep_row(0, 0, row(a_src, my_row), row(a_dst, me))
    for copy in tables:
        copy.wait()
    spot = lax.broadcasted_iota(jnp.int32, (owned * n, n), 0)
    piece = sum([jnp.where(spot >= n * j, 1, 0) for j in range(1, owned)])
    named = owned * (spot - n * piece) + piece
    pick = jnp.concatenate(
        [
            jnp.where(row_ref[l : l + 1, :] == named, sign_ref[l : l + 1, :], 0).astype(F32)
            for l in range(refs)
        ],
        axis=1,
    ).astype(BF16)
    arrive(0, a_dst)
    wanted = lax.dot_general(
        pick, stack_lanes(a_dst[...], length).astype(BF16), TN, preferred_element_type=F32
    )
    b_src[...] = spread_rows(wanted, refs)

    for arrival, span in ((1, (0, far)), (8, (far, n - 1))):
        send_rows(
            1, arrival, span, ahead, lambda k, peer: row(b_src, peer), lambda k: row(b_dst, k)
        )
    keep_row(1, 8, row(b_src, me), row(b_dst, n - 1))
    load.wait()
    for arrival, low, high, last in ((8, far, n, n - 1), (1, 0, far, far)):
        arrive(arrival, b_dst.at[pl.ds(low, high - low), :])
        c_src[low:high, :] = lax.dot_general(
            b_dst[low:high, :].astype(BF16), flex[...], NT, preferred_element_type=F32
        )
        send_rows(
            2, 2, (low, last), behind, lambda k, peer: row(c_src, k), lambda k: row(c_dst, me)
        )
    keep_row(2, 2, row(c_src, n - 1), row(c_dst, me))
    arrive(2, c_dst)
    terms = stack_lanes(c_dst[...], length)
    high, rest = halves(terms)
    middle, low = halves(terms - high.astype(F32))
    total = sum(
        [lax.dot_general(pick, t, NN, preferred_element_type=F32) for t in (low, middle, high)]
    )
    d_src[...] = spread_rows(total, owned)

    mine = full.at[col]
    for arrival, span in ((3, (0, far)), (9, (far, n - 1))):
        send_rows(
            3, arrival, span, ahead, lambda k, peer: row(d_src, peer), lambda k: row(mine, my_row)
        )
    keep_row(3, 9, row(d_src, me), row(mine, my_row))
    for arrival, count, group_dz in ((9, n - far, (0, 1, 7, 2, 6)), (3, far, (3, 5, 4))):
        arrive(arrival, mine.at[pl.ds(0, count), :])
        for dz in group_dz:
            z = lax.rem(my_z + dz, RING)
            part = mine.at[pl.ds(pl.multiple_of(z * plane, plane), plane), :]
            for dy in (2, 1, 3):
                pltpu.make_async_remote_copy(
                    src_ref=part, dst_ref=part, send_sem=send.at[4], recv_sem=recv.at[4],
                    device_id={"col": lax.rem(col + dy, m)}, device_id_type=MESH,
                ).start()
    arrive(4, full.at[pl.ds(0, m - 1)])
    whole = full[...].reshape(m * rows, width)
    full_ref[...] = whole
    g_src[...] = mm3(full[col], whole, NT)

    group = rows // plane
    pltpu.make_async_copy(
        g_src.at[pl.ds(my_part * group, group), :], g_dst.at[my_part], recv.at[5]
    ).start()
    for _, dx, core in plane_mates[-(plane - 1) :]:
        part = lax.rem(my_x + dx, across) * PAIR + lax.rem(my_core + core, PAIR)
        pltpu.make_async_remote_copy(
            src_ref=g_src.at[pl.ds(part * group, group), :], dst_ref=g_dst.at[my_part],
            send_sem=send.at[5], recv_sem=recv.at[5], device_id_type=MESH,
            device_id={"sub": at(my_x + dx, my_z, my_core + core)},
        ).start()
    arrive(5, g_dst)
    h_src[...] = jnp.sum(g_dst[...], axis=0)

    pltpu.make_async_copy(h_src, h_dst.at[my_z], recv.at[6]).start()
    for dz in (4, 3, 5, 2, 6, 1, 7):
        pltpu.make_async_remote_copy(
            src_ref=h_src, dst_ref=h_dst.at[my_z], send_sem=send.at[6], recv_sem=recv.at[6],
            device_id={"sub": at(my_x, my_z + dz, my_core)}, device_id_type=MESH,
        ).start()
    arrive(6, h_dst)
    i_src[...] = jnp.sum(h_dst[...], axis=0) / (width * n)

    place = gram.at[col * plane + my_part]
    pltpu.make_async_copy(i_src, place, recv.at[7]).start()
    for dy, dx, core in plane_mates:
        pltpu.make_async_remote_copy(
            src_ref=i_src, dst_ref=place, send_sem=send.at[7], recv_sem=recv.at[7],
            device_id={"sub": at(my_x + dx, my_z, my_core + core), "col": lax.rem(col + dy, m)},
            device_id_type=MESH,
        ).start()
    arrive(7, gram)
    gram_ref[...] = gram[...].reshape(m * rows, m * rows)

    for phase, sent in (
        (0, a_src), (1, b_src), (2, c_src), (3, d_src), (4, full.at[pl.ds(0, m - 1)]),
        (5, g_dst.at[pl.ds(0, plane - 1)]), (6, h_dst.at[pl.ds(0, RING - 1)]),
        (7, gram.at[pl.ds(0, m * plane - 1)]),
    ):
        pltpu.make_async_copy(sent, sent, send.at[phase]).wait()


def sketch_and_gram(omega, flexibility, block_row, block_sign):
    n, m = lax.axis_size("sub"), lax.axis_size("col")
    rows, width = omega.shape
    dofs = flexibility.shape[0]
    order = m * rows
    plane = n // RING
    group = rows // plane
    vmem = pl.BlockSpec(memory_space=pltpu.VMEM)
    return pl.pallas_call(
        functools.partial(sketch_kernel, n, m),
        out_shape=(
            jax.ShapeDtypeStruct((order, width), F32),
            jax.ShapeDtypeStruct((order, order), F32),
        ),
        in_specs=[pl.BlockSpec(memory_space=pltpu.HBM)] * 4,
        out_specs=(vmem, vmem),
        scratch_shapes=[
            pltpu.VMEM(omega.shape, omega.dtype),
            pltpu.VMEM(block_row.shape[::-1], jnp.int32),
            pltpu.VMEM(block_row.shape[::-1], jnp.int32),
            pltpu.SemaphoreType.DMA((3,)),
            pltpu.VMEM((8, 1, dofs), F32),
            pltpu.VMEM((dofs, dofs), BF16),
            pltpu.VMEM((rows, width), F32),
            pltpu.VMEM((n, width), F32),
            pltpu.VMEM((n, dofs), F32),
            pltpu.VMEM((rows, dofs), F32),
            pltpu.VMEM((rows, dofs), F32),
            pltpu.VMEM((n, dofs), F32),
            pltpu.VMEM((n, width), F32),
            pltpu.VMEM((m, rows, width), F32),
            pltpu.VMEM((rows, order), F32),
            pltpu.VMEM((plane, group, order), F32),
            pltpu.VMEM((group, order), F32),
            pltpu.VMEM((RING, group, order), F32),
            pltpu.VMEM((group, order), F32),
            pltpu.VMEM((m * plane, group, order), F32),
            pltpu.SemaphoreType.DMA,
            pltpu.SemaphoreType.DMA((8,)),
            pltpu.SemaphoreType.DMA((10,)),
        ],
        compiler_params=pltpu.CompilerParams(
            collective_id=0, has_side_effects=True, vmem_limit_bytes=12 << 20
        ),
        name="sketch_and_gram",
    )(*(pltpu.with_memory_space_constraint(x, pltpu.HBM) for x in (omega, flexibility, block_row.T, block_sign.T)))


def shards(flexibility, omega, block_row, block_sign):
    full, gram = sketch_and_gram(omega, flexibility[0], block_row, block_sign)
    return finish(full, gram, omega.shape[0])


def solution(mesh):
    placed = (P("sub", None, None), P("col", "sub"), P(), P())
    return jax.shard_map(
        shards,
        mesh=mesh,
        in_specs=placed,
        out_specs=(P("col", "sub"), P("col", "sub"), P()),
        check_vma=False,
    )
```

```python
import functools

import jax
import jax.numpy as jnp
from jax import lax
from jax.experimental import pallas as pl
from jax.experimental.pallas import tpu as pltpu
from jax.sharding import PartitionSpec as P

F32 = jnp.float32
BF16 = jnp.bfloat16
NN = (((1,), (0,)), ((), ()))
NT = (((1,), (1,)), ((), ()))


def mm1(a, b, dims=NN):
    return lax.dot_general(a.astype(BF16), b.astype(BF16), dims, preferred_element_type=F32)


def halves(a):
    high = a.astype(BF16)
    return high, (a - high.astype(F32)).astype(BF16)


def mm3(a, b, dims=NN):
    ah, al = halves(a)
    bh, bl = halves(b)
    dot = functools.partial(lax.dot_general, dimension_numbers=dims, preferred_element_type=F32)
    return dot(ah, bh) + (dot(ah, bl) + dot(al, bh))


def finish_kernel(full_ref, gram_ref, sketch_ref, basis_ref, upper_ref, work, lower):
    order = gram_ref.shape[0]
    rows = basis_ref.shape[0]
    i_row = lax.broadcasted_iota(jnp.int32, (order, order), 0)
    i_col = lax.broadcasted_iota(jnp.int32, (order, order), 1)
    eye = jnp.where(i_row == i_col, 1.0, 0.0).astype(F32)
    phi_mask = jnp.where(i_row > i_col, 1.0, 0.5 * eye).astype(F32)
    gram = gram_ref[...]
    on_diag = gram * eye
    d_row = jnp.sum(on_diag, axis=0, keepdims=True)
    d_col = jnp.sum(on_diag, axis=1, keepdims=True)
    s_row = lax.rsqrt(d_row)
    s_col = lax.rsqrt(d_col)
    err = jnp.where(i_row == i_col, 0.0, gram * s_row * s_col)
    p = err * phi_mask
    n = mm1(p, p, NT) * phi_mask + mm1(p, p) - p
    z = err + n + mm1(n, err)
    resid = z + n.T + mm1(z, n, NT)
    p = resid * phi_mask
    n = n - p - mm1(p, n)
    z = err + n + mm3(n, err)
    resid = z + n.T + mm3(z, n, NT)
    p = resid * phi_mask
    n = n - p - mm1(p, n)
    miss = jnp.sum(resid * resid)
    z = err + n + mm3(n, err)
    upper_ref[...] = jnp.where(i_row <= i_col, (eye + z) * (d_row * s_row), 0.0)
    lower[...] = jnp.where(i_row >= i_col, (eye + n) * s_row, 0.0)

    @pl.when(jnp.logical_not(miss < 4e-6))
    def eliminate():
        work[...] = gram
        lower[...] = eye
        lane = lax.broadcasted_iota(jnp.int32, (1, order), 1)
        sub = lax.broadcasted_iota(jnp.int32, (order, 1), 0)

        @pl.loop(0, order)
        def step(j):
            remain = work[...]
            row = work[pl.ds(j, 1), :]
            pivot = jnp.sum(jnp.where(lane == j, row, 0.0), axis=1, keepdims=True)
            scale = 1.0 / jnp.sqrt(pivot)
            u_row = jnp.where(lane >= j, row * scale, 0.0)
            column = jnp.sum(jnp.where(i_col == j, remain, 0.0), axis=1, keepdims=True)
            column = jnp.where(sub > j, column * scale, 0.0)
            l_row = lower[pl.ds(j, 1), :] * scale
            upper_ref[pl.ds(j, 1), :] = u_row
            work[...] = remain - column * u_row
            below = lower[...] - column * l_row
            lower[...] = jnp.where(sub == j, l_row, below)

    mine = pl.ds(pl.multiple_of(lax.axis_index("col") * rows, rows), rows)
    basis_ref[...] = mm3(lower[mine, :], full_ref[...])
    sketch_ref[...] = full_ref[mine, :]


def finish(full, gram, rows):
    order, width = full.shape
    return pl.pallas_call(
        finish_kernel,
        out_shape=(
            jax.ShapeDtypeStruct((rows, width), F32),
            jax.ShapeDtypeStruct((rows, width), F32),
            jax.ShapeDtypeStruct((order, order), F32),
        ),
        in_specs=[pl.BlockSpec(memory_space=pltpu.VMEM)] * 2,
        out_specs=(pl.BlockSpec(memory_space=pltpu.VMEM),) * 3,
        scratch_shapes=[pltpu.VMEM((order, order), F32)] * 2,
        compiler_params=pltpu.CompilerParams(vmem_limit_bytes=12 << 20),
        name="factor_and_basis",
    )(full, gram)


MESH = pl.DeviceIdType.MESH
RING = 8
PAIR = 2
SEATS = 8
TN = (((0,), (0,)), ((), ()))


def stack_lanes(x, length):
    return jnp.concatenate([x[:, k : k + length] for k in range(0, x.shape[1], length)], axis=0)


def spread_rows(x, parts):
    length = x.shape[0] // parts
    return jnp.concatenate([x[k * length : (k + 1) * length] for k in range(parts)], axis=1)


def centre_out(i, size):
    half = lax.div(i + 1, 2)
    return size // 2 + half * (1 - 2 * lax.rem(i, 2))


def sketch_kernel(
    n, m, omega_hbm, flex_ref, row_hbm, sign_hbm, full_ref, gram_ref,
    omega_ref, row_ref, sign_ref, load_sem, spare, spare_half, flex, a_src, a_dst, b_src, b_dst, c_src, c_dst, d_src, full, g_src, g_dst, h_src, h_dst, i_src, gram,
    flex_sem, send, recv,
):
    me = lax.axis_index("sub")
    col = lax.axis_index("col")
    rows, width = a_src.shape
    refs = row_ref.shape[0]
    length = c_src.shape[1] // refs
    owned = width // length

    across = n // (RING * PAIR)
    plane = across * PAIR
    my_x = lax.div(me, RING * PAIR)
    my_z = lax.rem(lax.div(me, PAIR), RING)
    my_core = lax.rem(me, PAIR)
    my_part = my_x * PAIR + my_core

    def at(x, z, core):
        x, z, core = lax.rem(x, across), lax.rem(z, RING), lax.rem(core, PAIR)
        return (x * RING + z) * PAIR + core

    def peer_of(k):
        in_plane = lax.rem(k, plane)
        dz = centre_out(lax.div(k, plane), RING)
        dx = centre_out(lax.div(in_plane, PAIR), across)
        return at(my_x + dx, my_z + dz, my_core + 1 - lax.rem(in_plane, PAIR))

    plane_mates = [
        (dy, dx, core)
        for dy in (2, 1, 3, 0)
        for dx in (2, 1, 3, 0)
        for core in (1, 0)
        if (dy, dx, core) != (0, 0, 0)
    ]
    barrier = pltpu.get_barrier_semaphore()

    def greet(k, carry):
        pl.semaphore_signal(
            barrier, inc=1, device_id={"sub": peer_of(k)}, device_id_type=MESH
        )
        return carry

    lax.fori_loop(0, n - 1, greet, 0)
    others = [mate for mate in plane_mates if mate[0]]
    for dy, dx, core in others:
        pl.semaphore_signal(
            barrier, inc=1, device_id_type=MESH,
            device_id={"sub": at(my_x + dx, my_z, my_core + core), "col": lax.rem(col + dy, m)},
        )
    tables = [
        pltpu.make_async_copy(row_hbm, row_ref, load_sem.at[1]),
        pltpu.make_async_copy(sign_hbm, sign_ref, load_sem.at[2]),
    ]
    load = pltpu.make_async_copy(flex_ref, flex, flex_sem)
    first = pltpu.make_async_copy(omega_hbm, omega_ref, load_sem.at[0])
    for copy in [first, *tables, load]:
        copy.start()
    first.wait()
    a_src[...] = omega_ref[...].astype(F32)
    pl.semaphore_wait(barrier, n - 1 + len(others))

    def start(phase, source, target, unread=None):
        own = pltpu.make_async_copy(source(me), target, recv.at[phase])
        own.start()
        pltpu.make_async_copy(
            source(me),
            spare.at[phase, :, pl.ds(0, target.shape[1])] if unread is None else unread,
            send.at[phase],
        ).start()

        def put(k, carry):
            peer = peer_of(k)
            pltpu.make_async_remote_copy(
                src_ref=source(peer), dst_ref=target, send_sem=send.at[phase],
                recv_sem=recv.at[phase], device_id={"sub": peer}, device_id_type=MESH,
            ).start()
            return carry

        lax.fori_loop(0, n - 1, put, 0)

    def arrive(phase, whole):
        pltpu.make_async_copy(whole, whole, recv.at[phase]).wait()

    def start_col(phase, ref):
        for k in range(1, m):
            pltpu.make_async_remote_copy(
                src_ref=ref.at[col], dst_ref=ref.at[col], send_sem=send.at[phase],
                recv_sem=recv.at[phase], device_id={"col": lax.rem(col + k, m)},
                device_id_type=MESH,
            ).start()

    def row_of(ref):
        return lambda r: ref.at[pl.ds(r, 1), :]

    start(0, row_of(a_src), a_dst.at[pl.ds(me, 1), :])
    for copy in tables:
        copy.wait()
    spot = lax.broadcasted_iota(jnp.int32, (owned * n, n), 0)
    piece = sum([jnp.where(spot >= n * j, 1, 0) for j in range(1, owned)])
    named = owned * (spot - n * piece) + piece
    pick = jnp.concatenate(
        [
            jnp.where(row_ref[l : l + 1, :] == named, sign_ref[l : l + 1, :], 0).astype(F32)
            for l in range(refs)
        ],
        axis=1,
    ).astype(BF16)
    held = lax.broadcasted_iota(jnp.int32, (refs * n, SEATS * n), 0)
    block = sum([jnp.where(held >= n * l, 1, 0) for l in range(1, refs)])
    seat = SEATS * (held - n * block) + block
    seat = jnp.where(lax.broadcasted_iota(jnp.int32, seat.shape, 1) == seat, 1.0, 0.0)
    seat = seat.astype(F32).astype(BF16)
    seated = lax.dot_general(pick, seat, NN, preferred_element_type=F32).astype(BF16)
    arrive(0, a_dst)
    wanted = lax.dot_general(
        seated, stack_lanes(a_dst[...], length).astype(BF16), TN, preferred_element_type=F32
    )
    b_src[...] = wanted.astype(BF16)

    def seats_of(ref):
        return lambda r: ref.at[pl.ds(pl.multiple_of(r * SEATS, SEATS), SEATS), :]

    start(1, seats_of(b_src), seats_of(b_dst)(me), spare_half)
    load.wait()
    arrive(1, b_dst)
    signed = lax.dot_general(seat, b_dst[...], NN, preferred_element_type=F32)
    c_src[...] = lax.dot_general(
        spread_rows(signed.astype(BF16), refs), flex[...], NT, preferred_element_type=F32
    )

    start(2, row_of(c_src), c_dst.at[pl.ds(me, 1), :])
    arrive(2, c_dst)
    terms = stack_lanes(c_dst[...], length)
    high, rest = halves(terms)
    middle, low = halves(terms - high.astype(F32))
    total = sum(
        [lax.dot_general(pick, t, NN, preferred_element_type=F32) for t in (low, middle, high)]
    )
    d_src[...] = spread_rows(total, owned)

    start(3, row_of(d_src), full.at[col, pl.ds(me, 1), :])
    arrive(3, full.at[col])
    start_col(4, full)
    arrive(4, full.at[pl.ds(0, m - 1)])
    whole = full[...].reshape(m * rows, width)
    full_ref[...] = whole
    g_src[...] = mm3(full[col], whole, NT)

    group = rows // plane
    pltpu.make_async_copy(
        g_src.at[pl.ds(my_part * group, group), :], g_dst.at[my_part], recv.at[5]
    ).start()
    for _, dx, core in plane_mates[-(plane - 1) :]:
        part = lax.rem(my_x + dx, across) * PAIR + lax.rem(my_core + core, PAIR)
        pltpu.make_async_remote_copy(
            src_ref=g_src.at[pl.ds(part * group, group), :], dst_ref=g_dst.at[my_part],
            send_sem=send.at[5], recv_sem=recv.at[5], device_id_type=MESH,
            device_id={"sub": at(my_x + dx, my_z, my_core + core)},
        ).start()
    arrive(5, g_dst)
    h_src[...] = jnp.sum(g_dst[...], axis=0)

    pltpu.make_async_copy(h_src, h_dst.at[my_z], recv.at[6]).start()
    for dz in (4, 3, 5, 2, 6, 1, 7):
        pltpu.make_async_remote_copy(
            src_ref=h_src, dst_ref=h_dst.at[my_z], send_sem=send.at[6], recv_sem=recv.at[6],
            device_id={"sub": at(my_x, my_z + dz, my_core)}, device_id_type=MESH,
        ).start()
    arrive(6, h_dst)
    i_src[...] = jnp.sum(h_dst[...], axis=0) / (width * n)

    place = gram.at[col * plane + my_part]
    pltpu.make_async_copy(i_src, place, recv.at[7]).start()
    for dy, dx, core in plane_mates:
        pltpu.make_async_remote_copy(
            src_ref=i_src, dst_ref=place, send_sem=send.at[7], recv_sem=recv.at[7],
            device_id={"sub": at(my_x + dx, my_z, my_core + core), "col": lax.rem(col + dy, m)},
            device_id_type=MESH,
        ).start()
    arrive(7, gram)
    gram_ref[...] = gram[...].reshape(m * rows, m * rows)

    for phase, sent in (
        (0, a_src), (1, b_src), (2, c_src), (3, d_src), (4, full.at[pl.ds(0, m - 1)]),
        (5, g_dst.at[pl.ds(0, plane - 1)]), (6, h_dst.at[pl.ds(0, RING - 1)]),
        (7, gram.at[pl.ds(0, m * plane - 1)]),
    ):
        pltpu.make_async_copy(sent, sent, send.at[phase]).wait()


def sketch_and_gram(omega, flexibility, block_row, block_sign):
    n, m = lax.axis_size("sub"), lax.axis_size("col")
    rows, width = omega.shape
    dofs = flexibility.shape[0]
    length = dofs // block_row.shape[1]
    order = m * rows
    plane = n // RING
    group = rows // plane
    vmem = pl.BlockSpec(memory_space=pltpu.VMEM)
    return pl.pallas_call(
        functools.partial(sketch_kernel, n, m),
        out_shape=(
            jax.ShapeDtypeStruct((order, width), F32),
            jax.ShapeDtypeStruct((order, order), F32),
        ),
        in_specs=[pl.BlockSpec(memory_space=pltpu.HBM)] * 4,
        out_specs=(vmem, vmem),
        scratch_shapes=[
            pltpu.VMEM(omega.shape, omega.dtype),
            pltpu.VMEM(block_row.shape[::-1], jnp.int32),
            pltpu.VMEM(block_row.shape[::-1], jnp.int32),
            pltpu.SemaphoreType.DMA((3,)),
            pltpu.VMEM((8, 1, dofs), F32),
            pltpu.VMEM((SEATS, length), BF16),
            pltpu.VMEM((dofs, dofs), BF16),
            pltpu.VMEM((rows, width), F32),
            pltpu.VMEM((n, width), F32),
            pltpu.VMEM((n * SEATS, length), BF16),
            pltpu.VMEM((n * SEATS, length), BF16),
            pltpu.VMEM((rows, dofs), F32),
            pltpu.VMEM((n, dofs), F32),
            pltpu.VMEM((n, width), F32),
            pltpu.VMEM((m, rows, width), F32),
            pltpu.VMEM((rows, order), F32),
            pltpu.VMEM((plane, group, order), F32),
            pltpu.VMEM((group, order), F32),
            pltpu.VMEM((RING, group, order), F32),
            pltpu.VMEM((group, order), F32),
            pltpu.VMEM((m * plane, group, order), F32),
            pltpu.SemaphoreType.DMA,
            pltpu.SemaphoreType.DMA((8,)),
            pltpu.SemaphoreType.DMA((8,)),
        ],
        compiler_params=pltpu.CompilerParams(
            collective_id=0, has_side_effects=True, vmem_limit_bytes=12 << 20
        ),
        name="sketch_and_gram",
    )(*(pltpu.with_memory_space_constraint(x, pltpu.HBM) for x in (omega, flexibility, block_row.T, block_sign.T)))


def shards(flexibility, omega, block_row, block_sign):
    full, gram = sketch_and_gram(omega, flexibility[0], block_row, block_sign)
    return finish(full, gram, omega.shape[0])


def solution(mesh):
    placed = (P("sub", None, None), P("col", "sub"), P(), P())
    return jax.shard_map(
        shards,
        mesh=mesh,
        in_specs=placed,
        out_specs=(P("col", "sub"), P("col", "sub"), P()),
        check_vma=False,
    )
```

```python
import functools

import jax
import jax.numpy as jnp
from jax import lax
from jax.experimental import pallas as pl
from jax.experimental.pallas import tpu as pltpu
from jax.sharding import PartitionSpec as P

F32 = jnp.float32
BF16 = jnp.bfloat16
NN = (((1,), (0,)), ((), ()))
NT = (((1,), (1,)), ((), ()))


def mm1(a, b, dims=NN):
    return lax.dot_general(a.astype(BF16), b.astype(BF16), dims, preferred_element_type=F32)


def halves(a):
    high = a.astype(BF16)
    return high, (a - high.astype(F32)).astype(BF16)


def mm3(a, b, dims=NN):
    ah, al = halves(a)
    bh, bl = halves(b)
    dot = functools.partial(lax.dot_general, dimension_numbers=dims, preferred_element_type=F32)
    return dot(ah, bh) + (dot(ah, bl) + dot(al, bh))


def finish_kernel(full_ref, gram_ref, sketch_ref, basis_ref, upper_ref, work, lower):
    order = gram_ref.shape[0]
    rows = basis_ref.shape[0]
    i_row = lax.broadcasted_iota(jnp.int32, (order, order), 0)
    i_col = lax.broadcasted_iota(jnp.int32, (order, order), 1)
    eye = jnp.where(i_row == i_col, 1.0, 0.0).astype(F32)
    phi_mask = jnp.where(i_row > i_col, 1.0, 0.5 * eye).astype(F32)
    gram = gram_ref[...]
    on_diag = gram * eye
    d_row = jnp.sum(on_diag, axis=0, keepdims=True)
    d_col = jnp.sum(on_diag, axis=1, keepdims=True)
    s_row = lax.rsqrt(d_row)
    s_col = lax.rsqrt(d_col)
    err = jnp.where(i_row == i_col, 0.0, gram * s_row * s_col)
    p = err * phi_mask
    n = mm1(p, p, NT) * phi_mask + mm1(p, p) - p
    z = err + n + mm1(n, err)
    resid = z + n.T + mm1(z, n, NT)
    p = resid * phi_mask
    n = n - p - mm1(p, n)
    z = err + n + mm3(n, err)
    resid = z + n.T + mm3(z, n, NT)
    p = resid * phi_mask
    change = p + mm1(p, n)
    miss = jnp.sum(resid * resid)
    n = n - change
    z = z - change - mm1(change, err)
    upper_ref[...] = jnp.where(i_row <= i_col, (eye + z) * (d_row * s_row), 0.0)
    lower[...] = jnp.where(i_row >= i_col, (eye + n) * s_row, 0.0)

    @pl.when(jnp.logical_not(miss < 4e-6))
    def eliminate():
        work[...] = gram
        lower[...] = eye
        lane = lax.broadcasted_iota(jnp.int32, (1, order), 1)
        sub = lax.broadcasted_iota(jnp.int32, (order, 1), 0)

        @pl.loop(0, order)
        def step(j):
            remain = work[...]
            row = work[pl.ds(j, 1), :]
            pivot = jnp.sum(jnp.where(lane == j, row, 0.0), axis=1, keepdims=True)
            scale = 1.0 / jnp.sqrt(pivot)
            u_row = jnp.where(lane >= j, row * scale, 0.0)
            column = jnp.sum(jnp.where(i_col == j, remain, 0.0), axis=1, keepdims=True)
            column = jnp.where(sub > j, column * scale, 0.0)
            l_row = lower[pl.ds(j, 1), :] * scale
            upper_ref[pl.ds(j, 1), :] = u_row
            work[...] = remain - column * u_row
            below = lower[...] - column * l_row
            lower[...] = jnp.where(sub == j, l_row, below)

    mine = pl.ds(pl.multiple_of(lax.axis_index("col") * rows, rows), rows)
    basis_ref[...] = mm3(lower[mine, :], full_ref[...])
    sketch_ref[...] = full_ref[mine, :]


def finish(full, gram, rows):
    order, width = full.shape
    return pl.pallas_call(
        finish_kernel,
        out_shape=(
            jax.ShapeDtypeStruct((rows, width), F32),
            jax.ShapeDtypeStruct((rows, width), F32),
            jax.ShapeDtypeStruct((order, order), F32),
        ),
        in_specs=[pl.BlockSpec(memory_space=pltpu.VMEM)] * 2,
        out_specs=(pl.BlockSpec(memory_space=pltpu.VMEM),) * 3,
        scratch_shapes=[pltpu.VMEM((order, order), F32)] * 2,
        compiler_params=pltpu.CompilerParams(vmem_limit_bytes=12 << 20),
        name="factor_and_basis",
    )(full, gram)


MESH = pl.DeviceIdType.MESH
RING = 8
PAIR = 2
SEATS = 8
TN = (((0,), (0,)), ((), ()))


def stack_lanes(x, length):
    return jnp.concatenate([x[:, k : k + length] for k in range(0, x.shape[1], length)], axis=0)


def spread_rows(x, parts):
    length = x.shape[0] // parts
    return jnp.concatenate([x[k * length : (k + 1) * length] for k in range(parts)], axis=1)


def centre_out(i, size):
    half = (i + 1) // 2
    return size // 2 + half * (1 - 2 * (i % 2))


def sketch_kernel(
    n, m, omega_hbm, flex_ref, row_hbm, sign_hbm, full_ref, gram_ref,
    omega_ref, row_ref, sign_ref, load_sem, spare, spare_half, flex, a_src, a_dst, b_src, b_dst, c_src, c_dst, d_src, full, g_src, g_dst, h_src, h_dst, i_src, gram,
    flex_sem, send, recv,
):
    me = lax.axis_index("sub")
    col = lax.axis_index("col")
    rows, width = a_src.shape
    refs = row_ref.shape[0]
    length = c_src.shape[1] // refs
    owned = width // length

    across = n // (RING * PAIR)
    plane = across * PAIR
    my_x = lax.div(me, RING * PAIR)
    my_z = lax.rem(lax.div(me, PAIR), RING)
    my_core = lax.rem(me, PAIR)
    my_part = my_x * PAIR + my_core

    def at(x, z, core):
        x, z, core = lax.rem(x, across), lax.rem(z, RING), lax.rem(core, PAIR)
        return (x * RING + z) * PAIR + core

    def peer_of(k):
        in_plane = k % plane
        dz = centre_out(k // plane, RING)
        dx = centre_out(in_plane // PAIR, across)
        return at(my_x + dx, my_z + dz, my_core + 1 - in_plane % PAIR)

    plane_mates = [
        (dy, dx, core)
        for dy in (2, 1, 3, 0)
        for dx in (2, 1, 3, 0)
        for core in (1, 0)
        if (dy, dx, core) != (0, 0, 0)
    ]
    barrier = pltpu.get_barrier_semaphore()

    def greet(k, carry):
        pl.semaphore_signal(
            barrier, inc=1, device_id={"sub": peer_of(k)}, device_id_type=MESH
        )
        return carry

    for k in range(n - 1):
        greet(k, 0)
    others = [mate for mate in plane_mates if mate[0]]
    for dy, dx, core in others:
        pl.semaphore_signal(
            barrier, inc=1, device_id_type=MESH,
            device_id={"sub": at(my_x + dx, my_z, my_core + core), "col": lax.rem(col + dy, m)},
        )
    tables = [
        pltpu.make_async_copy(row_hbm, row_ref, load_sem.at[1]),
        pltpu.make_async_copy(sign_hbm, sign_ref, load_sem.at[2]),
    ]
    load = pltpu.make_async_copy(flex_ref, flex, flex_sem)
    first = pltpu.make_async_copy(omega_hbm, omega_ref, load_sem.at[0])
    for copy in [first, *tables, load]:
        copy.start()
    first.wait()
    a_src[...] = omega_ref[...].astype(F32)
    pl.semaphore_wait(barrier, n - 1 + len(others))

    def start(phase, source, target, unread=None):
        def put(k, carry):
            peer = peer_of(k)
            pltpu.make_async_remote_copy(
                src_ref=source(peer), dst_ref=target, send_sem=send.at[phase],
                recv_sem=recv.at[phase], device_id={"sub": peer}, device_id_type=MESH,
            ).start()
            return carry

        for k in range(n - 1):
            put(k, 0)
        own = pltpu.make_async_copy(source(me), target, recv.at[phase])
        own.start()
        pltpu.make_async_copy(
            source(me),
            spare.at[phase, :, pl.ds(0, target.shape[1])] if unread is None else unread,
            send.at[phase],
        ).start()

    def arrive(phase, whole):
        pltpu.make_async_copy(whole, whole, recv.at[phase]).wait()

    def start_col(phase, ref):
        for k in range(1, m):
            pltpu.make_async_remote_copy(
                src_ref=ref.at[col], dst_ref=ref.at[col], send_sem=send.at[phase],
                recv_sem=recv.at[phase], device_id={"col": lax.rem(col + k, m)},
                device_id_type=MESH,
            ).start()

    def row_of(ref):
        return lambda r: ref.at[pl.ds(r, 1), :]

    start(0, row_of(a_src), a_dst.at[pl.ds(me, 1), :])
    for copy in tables:
        copy.wait()
    spot = lax.broadcasted_iota(jnp.int32, (owned * n, n), 0)
    piece = sum([jnp.where(spot >= n * j, 1, 0) for j in range(1, owned)])
    named = owned * (spot - n * piece) + piece
    pick = jnp.concatenate(
        [
            jnp.where(row_ref[l : l + 1, :] == named, sign_ref[l : l + 1, :], 0).astype(F32)
            for l in range(refs)
        ],
        axis=1,
    ).astype(BF16)
    held = lax.broadcasted_iota(jnp.int32, (refs * n, SEATS * n), 0)
    block = sum([jnp.where(held >= n * l, 1, 0) for l in range(1, refs)])
    seat = SEATS * (held - n * block) + block
    seat = jnp.where(lax.broadcasted_iota(jnp.int32, seat.shape, 1) == seat, 1.0, 0.0)
    seat = seat.astype(F32).astype(BF16)
    seated = lax.dot_general(pick, seat, NN, preferred_element_type=F32).astype(BF16)
    arrive(0, a_dst)
    wanted = lax.dot_general(
        seated, stack_lanes(a_dst[...], length).astype(BF16), TN, preferred_element_type=F32
    )
    b_src[...] = wanted.astype(BF16)

    def seats_of(ref):
        return lambda r: ref.at[pl.ds(pl.multiple_of(r * SEATS, SEATS), SEATS), :]

    start(1, seats_of(b_src), seats_of(b_dst)(me), spare_half)
    load.wait()
    arrive(1, b_dst)
    signed = lax.dot_general(seat, b_dst[...], NN, preferred_element_type=F32)
    c_src[...] = lax.dot_general(
        spread_rows(signed.astype(BF16), refs), flex[...], NT, preferred_element_type=F32
    )

    start(2, row_of(c_src), c_dst.at[pl.ds(me, 1), :])
    arrive(2, c_dst)
    terms = stack_lanes(c_dst[...], length)
    high, rest = halves(terms)
    middle, low = halves(terms - high.astype(F32))
    total = sum(
        [lax.dot_general(pick, t, NN, preferred_element_type=F32) for t in (low, middle, high)]
    )
    d_src[...] = spread_rows(total, owned)

    start(3, row_of(d_src), full.at[col, pl.ds(me, 1), :])
    arrive(3, full.at[col])
    start_col(4, full)
    arrive(4, full.at[pl.ds(0, m - 1)])
    whole = full[...].reshape(m * rows, width)
    full_ref[...] = whole
    g_src[...] = mm3(full[col], whole, NT)

    group = rows // plane
    for _, dx, core in plane_mates[-(plane - 1) :]:
        part = lax.rem(my_x + dx, across) * PAIR + lax.rem(my_core + core, PAIR)
        pltpu.make_async_remote_copy(
            src_ref=g_src.at[pl.ds(part * group, group), :], dst_ref=g_dst.at[my_part],
            send_sem=send.at[5], recv_sem=recv.at[5], device_id_type=MESH,
            device_id={"sub": at(my_x + dx, my_z, my_core + core)},
        ).start()
    pltpu.make_async_copy(
        g_src.at[pl.ds(my_part * group, group), :], g_dst.at[my_part], recv.at[5]
    ).start()
    arrive(5, g_dst)
    h_src[...] = jnp.sum(g_dst[...], axis=0)

    for dz in (4, 3, 5, 2, 6, 1, 7):
        pltpu.make_async_remote_copy(
            src_ref=h_src, dst_ref=h_dst.at[my_z], send_sem=send.at[6], recv_sem=recv.at[6],
            device_id={"sub": at(my_x, my_z + dz, my_core)}, device_id_type=MESH,
        ).start()
    pltpu.make_async_copy(h_src, h_dst.at[my_z], recv.at[6]).start()
    arrive(6, h_dst)
    i_src[...] = jnp.sum(h_dst[...], axis=0) / (width * n)

    place = gram.at[col * plane + my_part]
    for dy, dx, core in plane_mates:
        pltpu.make_async_remote_copy(
            src_ref=i_src, dst_ref=place, send_sem=send.at[7], recv_sem=recv.at[7],
            device_id={"sub": at(my_x + dx, my_z, my_core + core), "col": lax.rem(col + dy, m)},
            device_id_type=MESH,
        ).start()
    pltpu.make_async_copy(i_src, place, recv.at[7]).start()
    arrive(7, gram)
    gram_ref[...] = gram[...].reshape(m * rows, m * rows)

    for phase, sent in (
        (0, a_src), (1, b_src), (2, c_src), (3, d_src), (4, full.at[pl.ds(0, m - 1)]),
        (5, g_dst.at[pl.ds(0, plane - 1)]), (6, h_dst.at[pl.ds(0, RING - 1)]),
        (7, gram.at[pl.ds(0, m * plane - 1)]),
    ):
        pltpu.make_async_copy(sent, sent, send.at[phase]).wait()


def sketch_and_gram(omega, flexibility, block_row, block_sign):
    n, m = lax.axis_size("sub"), lax.axis_size("col")
    rows, width = omega.shape
    dofs = flexibility.shape[0]
    length = dofs // block_row.shape[1]
    order = m * rows
    plane = n // RING
    group = rows // plane
    vmem = pl.BlockSpec(memory_space=pltpu.VMEM)
    return pl.pallas_call(
        functools.partial(sketch_kernel, n, m),
        out_shape=(
            jax.ShapeDtypeStruct((order, width), F32),
            jax.ShapeDtypeStruct((order, order), F32),
        ),
        in_specs=[pl.BlockSpec(memory_space=pltpu.HBM)] * 4,
        out_specs=(vmem, vmem),
        scratch_shapes=[
            pltpu.VMEM(omega.shape, omega.dtype),
            pltpu.VMEM(block_row.shape[::-1], jnp.int32),
            pltpu.VMEM(block_row.shape[::-1], jnp.int32),
            pltpu.SemaphoreType.DMA((3,)),
            pltpu.VMEM((8, 1, dofs), F32),
            pltpu.VMEM((SEATS, length), BF16),
            pltpu.VMEM((dofs, dofs), BF16),
            pltpu.VMEM((rows, width), F32),
            pltpu.VMEM((n, width), F32),
            pltpu.VMEM((n * SEATS, length), BF16),
            pltpu.VMEM((n * SEATS, length), BF16),
            pltpu.VMEM((rows, dofs), F32),
            pltpu.VMEM((n, dofs), F32),
            pltpu.VMEM((n, width), F32),
            pltpu.VMEM((m, rows, width), F32),
            pltpu.VMEM((rows, order), F32),
            pltpu.VMEM((plane, group, order), F32),
            pltpu.VMEM((group, order), F32),
            pltpu.VMEM((RING, group, order), F32),
            pltpu.VMEM((group, order), F32),
            pltpu.VMEM((m * plane, group, order), F32),
            pltpu.SemaphoreType.DMA,
            pltpu.SemaphoreType.DMA((8,)),
            pltpu.SemaphoreType.DMA((8,)),
        ],
        compiler_params=pltpu.CompilerParams(
            collective_id=0, has_side_effects=True, vmem_limit_bytes=12 << 20
        ),
        name="sketch_and_gram",
    )(*(pltpu.with_memory_space_constraint(x, pltpu.HBM) for x in (omega, flexibility, block_row.T, block_sign.T)))


def shards(flexibility, omega, block_row, block_sign):
    full, gram = sketch_and_gram(omega, flexibility[0], block_row, block_sign)
    return finish(full, gram, omega.shape[0])


def solution(mesh):
    placed = (P("sub", None, None), P("col", "sub"), P(), P())
    return jax.shard_map(
        shards,
        mesh=mesh,
        in_specs=placed,
        out_specs=(P("col", "sub"), P("col", "sub"), P()),
        check_vma=False,
    )
```

```python
import functools

import jax
import jax.numpy as jnp
from jax import lax
from jax.experimental import pallas as pl
from jax.experimental.pallas import tpu as pltpu
from jax.sharding import PartitionSpec as P

F32 = jnp.float32
BF16 = jnp.bfloat16
NN = (((1,), (0,)), ((), ()))
NT = (((1,), (1,)), ((), ()))


def mm1(a, b, dims=NN):
    return lax.dot_general(a.astype(BF16), b.astype(BF16), dims, preferred_element_type=F32)


def halves(a):
    high = a.astype(BF16)
    return high, (a - high.astype(F32)).astype(BF16)


def mm3(a, b, dims=NN):
    ah, al = halves(a)
    bh, bl = halves(b)
    dot = functools.partial(lax.dot_general, dimension_numbers=dims, preferred_element_type=F32)
    return dot(ah, bh) + (dot(ah, bl) + dot(al, bh))


def finish_kernel(full_ref, gram_ref, sketch_ref, basis_ref, upper_ref, work, lower):
    order = gram_ref.shape[0]
    rows = basis_ref.shape[0]
    i_row = lax.broadcasted_iota(jnp.int32, (order, order), 0)
    i_col = lax.broadcasted_iota(jnp.int32, (order, order), 1)
    eye = jnp.where(i_row == i_col, 1.0, 0.0).astype(F32)
    phi_mask = jnp.where(i_row > i_col, 1.0, 0.5 * eye).astype(F32)
    gram = gram_ref[...]
    on_diag = gram * eye
    d_row = jnp.sum(on_diag, axis=0, keepdims=True)
    d_col = jnp.sum(on_diag, axis=1, keepdims=True)
    s_row = lax.rsqrt(d_row)
    s_col = lax.rsqrt(d_col)
    err = jnp.where(i_row == i_col, 0.0, gram * s_row * s_col)
    p = err * phi_mask
    n = mm1(p, p, NT) * phi_mask + mm1(p, p) - p
    z = err + n + mm1(n, err)
    resid = z + n.T + mm1(z, n, NT)
    p = resid * phi_mask
    n = n - p - mm1(p, n)
    z = err + n + mm3(n, err)
    resid = z + n.T + mm3(z, n, NT)
    p = resid * phi_mask
    change = p + mm1(p, n)
    miss = jnp.sum(resid * resid)
    n = n - change
    z = z - change - mm1(change, err)
    upper_ref[...] = jnp.where(i_row <= i_col, (eye + z) * (d_row * s_row), 0.0)
    lower[...] = jnp.where(i_row >= i_col, (eye + n) * s_row, 0.0)

    @pl.when(jnp.logical_not(miss < 4e-6))
    def eliminate():
        work[...] = gram
        lower[...] = eye
        lane = lax.broadcasted_iota(jnp.int32, (1, order), 1)
        sub = lax.broadcasted_iota(jnp.int32, (order, 1), 0)

        @pl.loop(0, order)
        def step(j):
            remain = work[...]
            row = work[pl.ds(j, 1), :]
            pivot = jnp.sum(jnp.where(lane == j, row, 0.0), axis=1, keepdims=True)
            scale = 1.0 / jnp.sqrt(pivot)
            u_row = jnp.where(lane >= j, row * scale, 0.0)
            column = jnp.sum(jnp.where(i_col == j, remain, 0.0), axis=1, keepdims=True)
            column = jnp.where(sub > j, column * scale, 0.0)
            l_row = lower[pl.ds(j, 1), :] * scale
            upper_ref[pl.ds(j, 1), :] = u_row
            work[...] = remain - column * u_row
            below = lower[...] - column * l_row
            lower[...] = jnp.where(sub == j, l_row, below)

    mine = pl.ds(pl.multiple_of(lax.axis_index("col") * rows, rows), rows)
    basis_ref[...] = mm3(lower[mine, :], full_ref[...])
    sketch_ref[...] = full_ref[mine, :]


def finish(full, gram, rows):
    order, width = full.shape
    return pl.pallas_call(
        finish_kernel,
        out_shape=(
            jax.ShapeDtypeStruct((rows, width), F32),
            jax.ShapeDtypeStruct((rows, width), F32),
            jax.ShapeDtypeStruct((order, order), F32),
        ),
        in_specs=[pl.BlockSpec(memory_space=pltpu.VMEM)] * 2,
        out_specs=(pl.BlockSpec(memory_space=pltpu.VMEM),) * 3,
        scratch_shapes=[pltpu.VMEM((order, order), F32)] * 2,
        compiler_params=pltpu.CompilerParams(vmem_limit_bytes=12 << 20),
        name="factor_and_basis",
    )(full, gram)


MESH = pl.DeviceIdType.MESH
RING = 8
PAIR = 2
SEATS = 8
TN = (((0,), (0,)), ((), ()))


def stack_lanes(x, length):
    return jnp.concatenate([x[:, k : k + length] for k in range(0, x.shape[1], length)], axis=0)


def spread_rows(x, parts):
    length = x.shape[0] // parts
    return jnp.concatenate([x[k * length : (k + 1) * length] for k in range(parts)], axis=1)


def centre_out(i, size):
    half = (i + 1) // 2
    return size // 2 + half * (1 - 2 * (i % 2))


def sketch_kernel(
    n, m, omega_hbm, flex_ref, row_hbm, sign_hbm, full_ref, gram_ref,
    omega_ref, row_ref, sign_ref, load_sem, spare, spare_half, flex, a_src, a_dst, b_src, b_dst, c_src, c_dst, d_src, full, g_src, g_dst, h_src, h_dst, i_src, gram,
    flex_sem, send, recv,
):
    me = lax.axis_index("sub")
    col = lax.axis_index("col")
    rows, width = a_src.shape
    refs = row_ref.shape[0]
    length = c_src.shape[1] // refs
    owned = width // length

    across = n // (RING * PAIR)
    plane = across * PAIR
    my_x = lax.div(me, RING * PAIR)
    my_z = lax.rem(lax.div(me, PAIR), RING)
    my_core = lax.rem(me, PAIR)
    my_part = my_x * PAIR + my_core

    def at(x, z, core):
        x, z, core = lax.rem(x, across), lax.rem(z, RING), lax.rem(core, PAIR)
        return (x * RING + z) * PAIR + core

    def peer_of(k):
        in_plane = k % plane
        dz = centre_out(k // plane, RING)
        dx = centre_out(in_plane // PAIR, across)
        return at(my_x + dx, my_z + dz, my_core + 1 - in_plane % PAIR)

    plane_mates = [
        (dy, dx, core)
        for dy in (2, 1, 3, 0)
        for dx in (2, 1, 3, 0)
        for core in (1, 0)
        if (dy, dx, core) != (0, 0, 0)
    ]
    barrier = pltpu.get_barrier_semaphore()

    def greet(k, carry):
        pl.semaphore_signal(
            barrier, inc=1, device_id={"sub": peer_of(k)}, device_id_type=MESH
        )
        return carry

    for k in range(n - 1):
        greet(k, 0)
    others = [mate for mate in plane_mates if mate[0]]
    for dy, dx, core in others:
        pl.semaphore_signal(
            barrier, inc=1, device_id_type=MESH,
            device_id={"sub": at(my_x + dx, my_z, my_core + core), "col": lax.rem(col + dy, m)},
        )
    tables = [
        pltpu.make_async_copy(row_hbm, row_ref, load_sem.at[1]),
        pltpu.make_async_copy(sign_hbm, sign_ref, load_sem.at[2]),
    ]
    load = pltpu.make_async_copy(flex_ref, flex, flex_sem)
    first = pltpu.make_async_copy(omega_hbm, omega_ref, load_sem.at[0])
    for copy in [first, *tables, load]:
        copy.start()
    first.wait()
    a_src[...] = omega_ref[...].astype(F32)
    pl.semaphore_wait(barrier, n - 1 + len(others))

    def start(phase, source, target, unread=None):
        def put(k, carry):
            peer = peer_of(k)
            pltpu.make_async_remote_copy(
                src_ref=source(peer), dst_ref=target, send_sem=send.at[phase],
                recv_sem=recv.at[phase], device_id={"sub": peer}, device_id_type=MESH,
            ).start()
            return carry

        for k in range(n - 1):
            put(k, 0)
        own = pltpu.make_async_copy(source(me), target, recv.at[phase])
        own.start()
        pltpu.make_async_copy(
            source(me),
            spare.at[phase, :, pl.ds(0, target.shape[1])] if unread is None else unread,
            send.at[phase],
        ).start()

    def arrive(phase, whole):
        pltpu.make_async_copy(whole, whole, recv.at[phase]).wait()

    def start_col(phase, ref):
        for k in sorted(range(1, m), key=lambda step: abs(step - m // 2)):
            pltpu.make_async_remote_copy(
                src_ref=ref.at[col], dst_ref=ref.at[col], send_sem=send.at[phase],
                recv_sem=recv.at[phase], device_id={"col": lax.rem(col + k, m)},
                device_id_type=MESH,
            ).start()

    def row_of(ref):
        return lambda r: ref.at[pl.ds(r, 1), :]

    start(0, row_of(a_src), a_dst.at[pl.ds(me, 1), :])
    for copy in tables:
        copy.wait()
    spot = lax.broadcasted_iota(jnp.int32, (owned * n, n), 0)
    piece = sum([jnp.where(spot >= n * j, 1, 0) for j in range(1, owned)])
    named = owned * (spot - n * piece) + piece
    pick = jnp.concatenate(
        [
            jnp.where(row_ref[l : l + 1, :] == named, sign_ref[l : l + 1, :], 0).astype(F32)
            for l in range(refs)
        ],
        axis=1,
    ).astype(BF16)
    held = lax.broadcasted_iota(jnp.int32, (refs * n, SEATS * n), 0)
    block = sum([jnp.where(held >= n * l, 1, 0) for l in range(1, refs)])
    seat = SEATS * (held - n * block) + block
    seat = jnp.where(lax.broadcasted_iota(jnp.int32, seat.shape, 1) == seat, 1.0, 0.0)
    seat = seat.astype(F32).astype(BF16)
    seated = lax.dot_general(pick, seat, NN, preferred_element_type=F32).astype(BF16)
    arrive(0, a_dst)
    wanted = lax.dot_general(
        seated, stack_lanes(a_dst[...], length).astype(BF16), TN, preferred_element_type=F32
    )
    b_src[...] = wanted.astype(BF16)

    def seats_of(ref):
        return lambda r: ref.at[pl.ds(pl.multiple_of(r * SEATS, SEATS), SEATS), :]

    start(1, seats_of(b_src), seats_of(b_dst)(me), spare_half)
    load.wait()
    arrive(1, b_dst)
    signed = lax.dot_general(seat, b_dst[...], NN, preferred_element_type=F32)
    c_src[...] = lax.dot_general(
        spread_rows(signed.astype(BF16), refs), flex[...], NT, preferred_element_type=F32
    )

    start(2, row_of(c_src), c_dst.at[pl.ds(me, 1), :])
    arrive(2, c_dst)
    terms = stack_lanes(c_dst[...], length)
    high, rest = halves(terms)
    middle, low = halves(terms - high.astype(F32))
    total = sum(
        [lax.dot_general(pick, t, NN, preferred_element_type=F32) for t in (low, middle, high)]
    )
    d_src[...] = spread_rows(total, owned)

    start(3, row_of(d_src), full.at[col, pl.ds(me, 1), :])
    arrive(3, full.at[col])
    start_col(4, full)
    arrive(4, full.at[pl.ds(0, m - 1)])
    whole = full[...].reshape(m * rows, width)
    full_ref[...] = whole
    g_src[...] = mm3(full[col], whole, NT)

    group = rows // plane
    for _, dx, core in plane_mates[-(plane - 1) :]:
        part = lax.rem(my_x + dx, across) * PAIR + lax.rem(my_core + core, PAIR)
        pltpu.make_async_remote_copy(
            src_ref=g_src.at[pl.ds(part * group, group), :], dst_ref=g_dst.at[my_part],
            send_sem=send.at[5], recv_sem=recv.at[5], device_id_type=MESH,
            device_id={"sub": at(my_x + dx, my_z, my_core + core)},
        ).start()
    pltpu.make_async_copy(
        g_src.at[pl.ds(my_part * group, group), :], g_dst.at[my_part], recv.at[5]
    ).start()
    arrive(5, g_dst)
    h_src[...] = jnp.sum(g_dst[...], axis=0)

    for dz in (4, 3, 5, 2, 6, 1, 7):
        pltpu.make_async_remote_copy(
            src_ref=h_src, dst_ref=h_dst.at[my_z], send_sem=send.at[6], recv_sem=recv.at[6],
            device_id={"sub": at(my_x, my_z + dz, my_core)}, device_id_type=MESH,
        ).start()
    pltpu.make_async_copy(h_src, h_dst.at[my_z], recv.at[6]).start()
    arrive(6, h_dst)
    i_src[...] = jnp.sum(h_dst[...], axis=0) / (width * n)

    place = gram.at[col * plane + my_part]
    for dy, dx, core in plane_mates:
        pltpu.make_async_remote_copy(
            src_ref=i_src, dst_ref=place, send_sem=send.at[7], recv_sem=recv.at[7],
            device_id={"sub": at(my_x + dx, my_z, my_core + core), "col": lax.rem(col + dy, m)},
            device_id_type=MESH,
        ).start()
    pltpu.make_async_copy(i_src, place, recv.at[7]).start()
    arrive(7, gram)
    gram_ref[...] = gram[...].reshape(m * rows, m * rows)

    for phase, sent in (
        (0, a_src), (1, b_src), (2, c_src), (3, d_src), (4, full.at[pl.ds(0, m - 1)]),
        (5, g_dst.at[pl.ds(0, plane - 1)]), (6, h_dst.at[pl.ds(0, RING - 1)]),
        (7, gram.at[pl.ds(0, m * plane - 1)]),
    ):
        pltpu.make_async_copy(sent, sent, send.at[phase]).wait()


def sketch_and_gram(omega, flexibility, block_row, block_sign):
    n, m = lax.axis_size("sub"), lax.axis_size("col")
    rows, width = omega.shape
    dofs = flexibility.shape[0]
    length = dofs // block_row.shape[1]
    order = m * rows
    plane = n // RING
    group = rows // plane
    vmem = pl.BlockSpec(memory_space=pltpu.VMEM)
    return pl.pallas_call(
        functools.partial(sketch_kernel, n, m),
        out_shape=(
            jax.ShapeDtypeStruct((order, width), F32),
            jax.ShapeDtypeStruct((order, order), F32),
        ),
        in_specs=[pl.BlockSpec(memory_space=pltpu.HBM)] * 4,
        out_specs=(vmem, vmem),
        scratch_shapes=[
            pltpu.VMEM(omega.shape, omega.dtype),
            pltpu.VMEM(block_row.shape[::-1], jnp.int32),
            pltpu.VMEM(block_row.shape[::-1], jnp.int32),
            pltpu.SemaphoreType.DMA((3,)),
            pltpu.VMEM((8, 1, dofs), F32),
            pltpu.VMEM((SEATS, length), BF16),
            pltpu.VMEM((dofs, dofs), BF16),
            pltpu.VMEM((rows, width), F32),
            pltpu.VMEM((n, width), F32),
            pltpu.VMEM((n * SEATS, length), BF16),
            pltpu.VMEM((n * SEATS, length), BF16),
            pltpu.VMEM((rows, dofs), F32),
            pltpu.VMEM((n, dofs), F32),
            pltpu.VMEM((n, width), F32),
            pltpu.VMEM((m, rows, width), F32),
            pltpu.VMEM((rows, order), F32),
            pltpu.VMEM((plane, group, order), F32),
            pltpu.VMEM((group, order), F32),
            pltpu.VMEM((RING, group, order), F32),
            pltpu.VMEM((group, order), F32),
            pltpu.VMEM((m * plane, group, order), F32),
            pltpu.SemaphoreType.DMA,
            pltpu.SemaphoreType.DMA((8,)),
            pltpu.SemaphoreType.DMA((8,)),
        ],
        compiler_params=pltpu.CompilerParams(
            collective_id=0, has_side_effects=True, vmem_limit_bytes=12 << 20
        ),
        name="sketch_and_gram",
    )(*(pltpu.with_memory_space_constraint(x, pltpu.HBM) for x in (omega, flexibility, block_row.T, block_sign.T)))


def shards(flexibility, omega, block_row, block_sign):
    full, gram = sketch_and_gram(omega, flexibility[0], block_row, block_sign)
    return finish(full, gram, omega.shape[0])


def solution(mesh):
    placed = (P("sub", None, None), P("col", "sub"), P(), P())
    return jax.shard_map(
        shards,
        mesh=mesh,
        in_specs=placed,
        out_specs=(P("col", "sub"), P("col", "sub"), P()),
        check_vma=False,
    )
```
